128 devices in a mesh: cluster: 8 (over x, core), row: 16 (over z, y).
Axes of the slice: x: 4, y: 4, z: 4, core: 2. Of those that a mesh axis runs over, the one named last changes fastest.
Arguments:
- sources: bfloat16 [32768, 512], P(('cluster', 'row')), may hold values from -12 to 12
- targets: bfloat16 [32768, 512], P(('cluster', 'row')), may hold values from -12 to 12
- source_order: int32 [32768], P(('cluster', 'row')), may hold values from 0 to 255, as said below
- target_order: int32 [32768], P(('cluster', 'row')), may hold values from 0 to 255, as said below
Outputs:
- source_map: bfloat16 [32768, 512], P(('cluster', 'row'))
- target_map: bfloat16 [32768, 512], P(('cluster', 'row'))
The draws below stay inside these ranges and needn't reach their ends.
Inputs may be any that keep to these rules, and one draw needn't show every extreme that they name: `source_order`: in each aligned block of 256 consecutive rows every value appears exactly once, so each block holds 32 source rows of every co-cluster. `target_order`: in each aligned block of 256 consecutive rows every value appears exactly once, so each block holds 32 target rows of every co-cluster.
All inputs are finite; a program needn't handle non-finite values.
Results may differ from the reference program's by a relative error of at most 0.01.
Values may be sent and summed in bfloat16 or wider, within the bound.
No kernel may reach another device: no remote copies, remote signals or barrier semaphores. Data moves between devices by JAX's collectives and lax.ppermute only.
A program may use at most 64 MiB of HBM per device.

```python
import math
import jax
import jax.numpy as jnp
from jax import lax

D = 512
ROWS_DEV = 256
ITERS = 3
CLUSTERS = 8
CPC = 4096
ROWS = 32768
PER = 32


def block_orders(key, salt):
    blocks = ROWS // ROWS_DEV
    subkeys = jax.random.split(jax.random.fold_in(key, salt), blocks)
    shuffled = jax.vmap(lambda subkey: jax.random.permutation(subkey, ROWS_DEV))(subkeys)
    return shuffled.reshape(-1).astype(jnp.int32)


def draw_source_order(key, part):
    return block_orders(key, 11)


def draw_target_order(key, part):
    return block_orders(key, 12)


def base_rows(key, salt):
    noise = jnp.clip(jax.random.normal(jax.random.fold_in(key, salt), (ROWS, D), jnp.float32), -5.0, 5.0)
    logs = jax.random.uniform(jax.random.fold_in(key, salt + 1), (ROWS, 1), jnp.float32, math.log(0.4), math.log(2.0))
    return noise * jnp.exp(logs)


def draw_sources(key, part):
    base = base_rows(key, 31)
    result = base
    return result.astype(jnp.bfloat16)


def draw_targets(key, part):
    base = base_rows(key, 41)
    result = base
    return result.astype(jnp.bfloat16)


def setup_inputs(seed: int = 0) -> dict:
    arg_keys = jax.random.split(jax.random.key(seed), 5)
    return {
        "sources": draw_sources(jax.random.fold_in(arg_keys[4], 71), 0),
        "targets": draw_targets(jax.random.fold_in(arg_keys[4], 71), 0),
        "source_order": draw_source_order(jax.random.fold_in(arg_keys[4], 71), 0),
        "target_order": draw_target_order(jax.random.fold_in(arg_keys[4], 71), 0),
    }


entropy_weight = 0.02


def square_sums(matrix):
    widened = matrix.astype(jnp.float32)
    return jnp.sum(widened * widened, axis=1)


def log_sum_exp(scores, axis):
    highest = jnp.max(scores, axis=axis, keepdims=True)
    return jnp.squeeze(highest, axis) + jnp.log(jnp.sum(jnp.exp(scores - highest), axis=axis))


def one_cluster(members):
    source_rows, target_rows = members
    inner = jnp.dot(source_rows, target_rows.T, preferred_element_type=jnp.float32)
    cost = (square_sums(source_rows)[:, None] + square_sums(target_rows)[None, :] - 2.0 * inner) / D
    log_mass = -math.log(CPC)
    target_potential = jnp.zeros((CPC,), jnp.float32)
    for repeat in range(ITERS):
        source_potential = entropy_weight * (log_mass - log_sum_exp((target_potential[None, :] - cost) / entropy_weight, 1))
        column_scores = (source_potential[:, None] - cost) / entropy_weight
        column_norm = log_sum_exp(column_scores, 0)
        target_potential = entropy_weight * (log_mass - column_norm)
    target_weight = jnp.exp(column_scores - column_norm[None, :]).astype(jnp.bfloat16)
    target_map = jnp.dot(target_weight.T, source_rows, preferred_element_type=jnp.float32).astype(jnp.bfloat16)
    row_scores = (target_potential[None, :] - cost) / entropy_weight
    row_norm = log_sum_exp(row_scores, 1)
    source_weight = jnp.exp(row_scores - row_norm[:, None]).astype(jnp.bfloat16)
    source_map = jnp.dot(source_weight, target_rows, preferred_element_type=jnp.float32).astype(jnp.bfloat16)
    return source_map, target_map


def reference(sources, targets, source_order, target_order):
    source_index = jnp.argsort(source_order // PER, stable=True).astype(jnp.int32).reshape(CLUSTERS, CPC)
    target_index = jnp.argsort(target_order // PER, stable=True).astype(jnp.int32).reshape(CLUSTERS, CPC)
    source_maps, target_maps = lax.map(one_cluster, (sources[source_index], targets[target_index]))
    source_map = jnp.zeros_like(sources).at[source_index.reshape(-1)].set(source_maps.reshape(-1, D))
    target_map = jnp.zeros_like(targets).at[target_index.reshape(-1)].set(target_maps.reshape(-1, D))
    return source_map, target_map
```

```python
import functools
import math

import jax
import jax.numpy as jnp
from jax import lax
from jax.experimental import pallas as pl
from jax.experimental.pallas import tpu as pltpu
from jax.sharding import Mesh, PartitionSpec as P

ITERS = 3
entropy_weight = 0.02
AXES = ("xh", "xl", "core", "zh", "zl", "yh", "yl")
CLUSTER = ("xh", "zh", "yh")
SWAP = [(0, 1), (1, 0)]
VMEM_LIMIT = 24 * 1024 * 1024
LANES = 128


def compact(column):
    rows = [
        jnp.transpose(jnp.broadcast_to(column[a : a + LANES], (LANES, LANES)))[0:1]
        for a in range(0, column.shape[0], LANES)
    ]
    return jnp.concatenate(rows, axis=0)


def combine(parts):
    highest = functools.reduce(jnp.maximum, parts)
    total = functools.reduce(jnp.add, [jnp.exp2(part - highest) for part in parts])
    return highest + jnp.log2(total)


def put_row(row_ref, value):
    for a in range(value.shape[0]):
        row_ref[0:1, a * LANES : (a + 1) * LANES] = value[a : a + 1]


def put_column(column_ref, value):
    for a in range(value.shape[0]):
        spread = jnp.transpose(jnp.broadcast_to(value[a : a + 1], (LANES, LANES)))
        column_ref[a * LANES : (a + 1) * LANES] = spread[:, 0:1]


def row_lse_chunk(scores):
    highest = jnp.max(scores, axis=1, keepdims=True)
    total = jnp.sum(jnp.exp2(scores - highest), axis=1, keepdims=True)
    return highest + jnp.log2(total)


def scores_kernel(scale, places, s0, s1, s2, s3, t0, t1, t2, t3, m_ref, x_ref, y_ref, lse_ref, norm_ref):
    rows, width = s0.shape
    for r, (s, t) in enumerate(zip((s0, s1, s2, s3), (t0, t1, t2, t3))):
        x_ref[pl.ds(pl.multiple_of((places[0] ^ r) * rows, rows), rows), :] = s[...]
        y_ref[pl.ds(pl.multiple_of((places[1] ^ r) * rows, rows), rows), :] = t[...]
    for a in range(0, y_ref.shape[0], LANES):
        wide = y_ref[a : a + LANES, :].astype(jnp.float32)
        square = wide * wide
        folded = functools.reduce(jnp.add, [square[:, c : c + LANES] for c in range(0, width, LANES)])
        norm_ref[0:1, a : a + LANES] = jnp.sum(jnp.transpose(folded), axis=0, keepdims=True)
    step = 128
    for a in range(0, x_ref.shape[0], step):
        block = x_ref[a : a + step, :]
        wide = block.astype(jnp.float32)
        norms = jnp.sum(wide * wide, axis=1, keepdims=True)
        inner = lax.dot_general(
            block, y_ref[...], (((1,), (1,)), ((), ())), preferred_element_type=jnp.float32
        )
        scores = (2.0 * inner - norms - norm_ref[...]) * scale
        m_ref[a : a + step, :] = scores
        lse_ref[a // LANES : a // LANES + 1, :] = compact(row_lse_chunk(scores))


def row_kernel(log_mass, m_ref, c0, lse_ref, row_ref):
    put_row(row_ref, log_mass - combine([c0[p] for p in range(4)]))
    step = 128
    for a in range(0, m_ref.shape[0], step):
        scores = m_ref[a : a + step, :] + row_ref[...]
        lse_ref[a // LANES : a // LANES + 1, :] = compact(row_lse_chunk(scores))


def column_kernel(log_mass, m_ref, own, mate, pair, lse_ref, f_ref, column_ref):
    potential = log_mass - combine([own[...], mate[...], pair[0], pair[1]])
    f_ref[...] = potential
    put_column(column_ref, potential)
    columns = m_ref.shape[1]
    step = 32

    def fold(values, op):
        return functools.reduce(op, [values[b : b + 8] for b in range(0, step, 8)])

    highest = jnp.full((8, columns), -jnp.inf, jnp.float32)
    for a in range(0, m_ref.shape[0], step):
        highest = jnp.maximum(highest, fold(m_ref[a : a + step, :] + column_ref[a : a + step], jnp.maximum))
    highest = jnp.max(highest, axis=0, keepdims=True)
    total = jnp.zeros((8, columns), jnp.float32)
    for a in range(0, m_ref.shape[0], step):
        scores = m_ref[a : a + step, :] + column_ref[a : a + step]
        total = total + fold(jnp.exp2(scores - highest), jnp.add)
    lse = highest + jnp.log2(jnp.sum(total, axis=0, keepdims=True))
    for a in range(lse_ref.shape[0]):
        lse_ref[a : a + 1, :] = lse[:, a * LANES : (a + 1) * LANES]


def target_kernel(m_ref, x_ref, f, c0, out_ref, column_ref, row_ref):
    put_column(column_ref, f[...])
    put_row(row_ref, combine([c0[p] for p in range(4)]))
    step = 256
    for a in range(0, m_ref.shape[1], step):
        scores = m_ref[:, a : a + step] + column_ref[...]
        weights = jnp.exp2(scores - row_ref[:, a : a + step]).astype(jnp.bfloat16)
        out_ref[a : a + step, :] = lax.dot_general(
            weights, x_ref[...], (((0,), (0,)), ((), ())), preferred_element_type=jnp.float32
        ).astype(jnp.bfloat16)


def source_kernel(log_mass, m_ref, y_ref, c0, out_ref, lse_ref, row_ref):
    put_row(row_ref, log_mass - combine([c0[p] for p in range(4)]))
    step = 128
    for a in range(0, m_ref.shape[0], step):
        scores = m_ref[a : a + step, :] + row_ref[...]
        highest = jnp.max(scores, axis=1, keepdims=True)
        raised = jnp.exp2(scores - highest)
        total = jnp.sum(raised, axis=1, keepdims=True)
        mapped = jnp.dot(raised.astype(jnp.bfloat16), y_ref[...], preferred_element_type=jnp.float32)
        out_ref[a : a + step, :] = mapped / total
        lse_ref[a // LANES : a // LANES + 1, :] = compact(highest + jnp.log2(total))


def scale_kernel(places, p_ref, lse_ref, own, mate, pair, out_ref, column_ref):
    rows = out_ref.shape[0] // 4
    put_column(column_ref, jnp.exp2(lse_ref[...] - combine([own[...], mate[...], pair[0], pair[1]])))
    for r in range(4):
        a = pl.multiple_of((places[0] ^ r) * rows, rows)
        out_ref[r * rows : (r + 1) * rows, :] = (
            p_ref[pl.ds(a, rows), :] * column_ref[pl.ds(a, rows), :]
        ).astype(jnp.bfloat16)


def into_slots(ordering, matrix):
    positions = jnp.arange(matrix.shape[0], dtype=jnp.int32)
    selector = (positions[:, None] == ordering[None, :]).astype(jnp.bfloat16)
    return jnp.dot(selector, matrix, preferred_element_type=jnp.float32).astype(jnp.bfloat16)


def out_of_slots(ordering, matrix):
    positions = jnp.arange(matrix.shape[0], dtype=jnp.int32)
    selector = (ordering[:, None] == positions[None, :]).astype(jnp.bfloat16)
    return jnp.dot(selector, matrix, preferred_element_type=jnp.float32).astype(jnp.bfloat16)


def swap(value, axis):
    return lax.ppermute(value, axis, SWAP)


def shards(sources, targets, source_order, target_order):
    rows, width = sources.shape
    side = 4 * rows
    per = rows // 8
    log_mass = -math.log2(4 * side)
    scale = 1.0 / (width * entropy_weight * math.log(2.0))
    vmem = pl.BlockSpec(memory_space=pltpu.VMEM)
    smem = pl.BlockSpec(memory_space=pltpu.SMEM)
    f32, bf16 = jnp.float32, jnp.bfloat16
    tile = (side // LANES, LANES)

    def held(shape, dtype):
        return pltpu.VMEM(shape, dtype)

    def plain(shape, dtype):
        return jax.ShapeDtypeStruct(shape, dtype)

    def call(kernel, outs, scratch, specs, flops):
        return pl.pallas_call(
            kernel,
            out_shape=outs,
            in_specs=specs,
            out_specs=[vmem] * len(outs),
            scratch_shapes=scratch,
            compiler_params=pltpu.CompilerParams(vmem_limit_bytes=VMEM_LIMIT),
            cost_estimate=pl.CostEstimate(flops=flops, bytes_accessed=4 * side * side, transcendentals=side * side),
        )

    sent = jnp.concatenate(
        [
            into_slots(source_order, sources).reshape(8, per, width),
            into_slots(target_order, targets).reshape(8, per, width),
        ],
        axis=1,
    )
    got = lax.all_to_all(sent, CLUSTER, split_axis=0, concat_axis=0, tiled=True)
    mine = got[:, :per].reshape(rows, width)
    aims = got[:, per:].reshape(rows, width)

    tx = swap(aims, "xl")
    ty = swap(aims, "yl")
    sz = swap(mine, "zl")
    sc = swap(mine, "core")
    half = rows // 2
    txy = jnp.concatenate([swap(ty[:half], "xl"), swap(tx[half:], "yl")], axis=0)
    scz = swap(sz, "core")
    places = jnp.stack(
        [
            lax.axis_index("core") * 2 + lax.axis_index("zl"),
            lax.axis_index("xl") * 2 + lax.axis_index("yl"),
        ]
    ).astype(jnp.int32)
    flops = 2 * side * side * width
    matrix, all_sources, all_targets, row_part = call(
        functools.partial(scores_kernel, scale),
        [plain((side, side), f32), plain((side, width), bf16), plain((side, width), bf16), plain(tile, f32)],
        [pltpu.VMEM((1, side), f32)],
        [smem] + [vmem] * 8,
        flops,
    )(places, mine, sz, sc, scz, aims, ty, tx, txy)

    def exchange_rows(part):
        mate = swap(part, "core")
        pair = swap(jnp.stack([part, mate]), "zl")
        return part, mate, pair

    def exchange_columns(part):
        spread = jnp.broadcast_to(part[None], (4,) + part.shape)
        return lax.all_to_all(spread, ("xl", "yl"), split_axis=0, concat_axis=0, tiled=True)

    for repeat in range(ITERS):
        row_parts = exchange_rows(row_part)
        column_part, potential = call(
            functools.partial(column_kernel, log_mass),
            [plain(tile, f32), plain(tile, f32)],
            [pltpu.VMEM((side, 1), f32)],
            [vmem] * 4,
            0,
        )(matrix, *row_parts)
        column_parts = exchange_columns(column_part)
        if repeat < ITERS - 1:
            (row_part,) = call(
                functools.partial(row_kernel, log_mass),
                [plain(tile, f32)],
                [pltpu.VMEM((1, side), f32)],
                [vmem] * 2,
                0,
            )(matrix, column_parts)

    (target_part,) = call(
        target_kernel,
        [plain((side, width), bf16)],
        [pltpu.VMEM((side, 1), f32), pltpu.VMEM((1, side), f32)],
        [vmem] * 4,
        flops,
    )(matrix, all_sources, potential, column_parts)
    source_part, row_part = call(
        functools.partial(source_kernel, log_mass),
        [plain((side, width), f32), plain(tile, f32)],
        [pltpu.VMEM((1, side), f32)],
        [vmem] * 3,
        flops,
    )(matrix, all_targets, column_parts)
    row_parts = exchange_rows(row_part)
    (scaled,) = call(
        scale_kernel,
        [plain((side, width), bf16)],
        [pltpu.VMEM((side, 1), f32)],
        [smem] + [vmem] * 5,
        0,
    )(places, source_part, row_part, *row_parts)
    near = swap(scaled[2 * rows :], "core")
    first = (scaled[: 2 * rows].astype(f32) + near.astype(f32)).astype(bf16)
    far = swap(first[rows:], "zl")
    source_map = (first[:rows].astype(f32) + far.astype(f32)).astype(bf16)
    target_pieces = lax.all_to_all(
        target_part.reshape(4, rows, width), ("xl", "yl"), split_axis=0, concat_axis=0, tiled=True
    )
    target_map = jnp.sum(target_pieces.astype(f32), axis=0).astype(bf16)
    back = jnp.concatenate(
        [source_map.reshape(8, per, width), target_map.reshape(8, per, width)], axis=1
    )
    back = lax.all_to_all(back, CLUSTER, split_axis=0, concat_axis=0, tiled=True)
    return (
        out_of_slots(source_order, back[:, :per].reshape(rows, width)),
        out_of_slots(target_order, back[:, per:].reshape(rows, width)),
    )


def solution(mesh):
    split = Mesh(mesh.devices.reshape((2,) * 7), AXES)
    return jax.shard_map(
        shards,
        mesh=split,
        in_specs=(P(AXES, None), P(AXES, None), P(AXES), P(AXES)),
        out_specs=(P(AXES, None), P(AXES, None)),
        check_vma=False,
    )
```

```python
import functools
import math

import jax
import jax.numpy as jnp
from jax import lax
from jax.experimental import pallas as pl
from jax.experimental.pallas import tpu as pltpu
from jax.sharding import Mesh, PartitionSpec as P

ITERS = 3
entropy_weight = 0.02
AXES = ("x", "core", "zh", "zl", "y")
SIZES = (4, 2, 2, 2, 4)
CLUSTER = ("x", "zh")
SWAP = [(0, 1), (1, 0)]
NEXT = [(i, i ^ 1) for i in range(4)]
LAST = [(i, i ^ 3) for i in range(4)]
ACROSS = [(i, i ^ 2) for i in range(4)]
VMEM_LIMIT = 24 * 1024 * 1024
LANES = 128
STEP = 128


def compact(column):
    rows = [
        jnp.transpose(jnp.broadcast_to(column[a : a + LANES], (LANES, LANES)))[0:1]
        for a in range(0, column.shape[0], LANES)
    ]
    return jnp.concatenate(rows, axis=0)


def combine(parts):
    highest = functools.reduce(jnp.maximum, parts)
    total = functools.reduce(jnp.add, [jnp.exp2(part - highest) for part in parts])
    return highest + jnp.log2(total)


def flip(part, q):
    per = part.shape[0] // 4
    return jnp.concatenate([part[(p ^ q) * per : ((p ^ q) + 1) * per] for p in range(4)], axis=0)


def aligned(parts):
    return [part if q == 0 else flip(part, q) for q, part in enumerate(parts)]


def put_row(row_ref, value):
    for a in range(value.shape[0]):
        row_ref[0:1, a * LANES : (a + 1) * LANES] = value[a : a + 1]


def put_column(column_ref, value):
    for a in range(value.shape[0]):
        spread = jnp.transpose(jnp.broadcast_to(value[a : a + 1], (LANES, LANES)))
        column_ref[a * LANES : (a + 1) * LANES] = spread[:, 0:1]


def row_lse_chunk(scores):
    highest = jnp.max(scores, axis=1, keepdims=True)
    total = jnp.sum(jnp.exp2(scores - highest), axis=1, keepdims=True)
    return highest + jnp.log2(total)


def pack_kernel(so_ref, s_ref, to_ref, t_ref, out_ref):
    rows = s_ref.shape[0]
    per = rows // 8
    slots = lax.broadcasted_iota(jnp.int32, (rows, rows), 0)
    for part, (order, matrix) in enumerate(((so_ref, s_ref), (to_ref, t_ref))):
        chosen = jnp.where(slots == order[...], 1.0, 0.0).astype(jnp.bfloat16)
        moved = jnp.dot(chosen, matrix[...], preferred_element_type=jnp.float32).astype(jnp.bfloat16)
        for k in range(8):
            out_ref[k, part * per : (part + 1) * per, :] = moved[k * per : (k + 1) * per]


def unpack_kernel(so_ref, to_ref, back_ref, s_ref, t_ref):
    rows = s_ref.shape[0]
    per = rows // 8
    slots = lax.broadcasted_iota(jnp.int32, (rows, rows), 0)
    for part, (order, out) in enumerate(((so_ref, s_ref), (to_ref, t_ref))):
        chosen = jnp.where(slots == order[...], 1.0, 0.0).astype(jnp.bfloat16)
        moved = back_ref[:, part * per : (part + 1) * per, :].reshape(rows, out.shape[1])
        out[...] = lax.dot_general(
            chosen, moved, (((0,), (0,)), ((), ())), preferred_element_type=jnp.float32
        ).astype(jnp.bfloat16)


def target_norms(norm_ref, block, start):
    width = block.shape[1]
    for a in range(0, block.shape[0], LANES):
        wide = block[a : a + LANES, :].astype(jnp.float32)
        square = wide * wide
        folded = functools.reduce(jnp.add, [square[:, c : c + LANES] for c in range(0, width, LANES)])
        norm_ref[0:1, start + a : start + a + LANES] = jnp.sum(jnp.transpose(folded), axis=0, keepdims=True)


def score_block(scale, block, norms, targets, target_row):
    inner = lax.dot_general(block, targets, (((1,), (1,)), ((), ())), preferred_element_type=jnp.float32)
    return (2.0 * inner - norms - target_row) * scale


def first_kernel(scale, s0, s1, s2, s3, t0, t1, t2, m_ref, x_ref, y_ref, lse_ref, sn_ref, norm_ref):
    rows = s0.shape[0]
    for q, s in enumerate((s0, s1, s2, s3)):
        x_ref[q * rows : (q + 1) * rows, :] = s[...]
    for q, t in enumerate((t0, t1, t2)):
        y_ref[q * rows : (q + 1) * rows, :] = t[...]
        target_norms(norm_ref, t, q * rows)
    ready = 3 * rows
    for a in range(0, x_ref.shape[0], STEP):
        block = x_ref[a : a + STEP, :]
        wide = block.astype(jnp.float32)
        norms = jnp.sum(wide * wide, axis=1, keepdims=True)
        sn_ref[a : a + STEP] = norms
        scores = score_block(scale, block, norms, y_ref[0:ready, :], norm_ref[...])
        m_ref[a : a + STEP, 0:ready] = scores
        lse_ref[a // LANES : a // LANES + 1, :] = compact(row_lse_chunk(scores))


def second_kernel(scale, x_ref, sn_ref, part_ref, t3, m_in, y_in, m_ref, y_ref, lse_ref, norm_ref):
    rows = t3.shape[0]
    ready = 3 * rows
    y_ref[ready : 4 * rows, :] = t3[...]
    target_norms(norm_ref, t3, 0)
    for a in range(0, x_ref.shape[0], STEP):
        scores = score_block(scale, x_ref[a : a + STEP, :], sn_ref[a : a + STEP], t3[...], norm_ref[...])
        m_ref[a : a + STEP, ready : 4 * rows] = scores
        g = a // LANES
        lse_ref[g : g + 1, :] = combine([part_ref[g : g + 1, :], compact(row_lse_chunk(scores))])


def row_kernel(log_mass, m_ref, own, mate, pair, lse_ref, g_ref, row_ref):
    potential = log_mass - combine(aligned([own[...], mate[...], pair[0], pair[1]]))
    g_ref[...] = potential
    put_row(row_ref, potential)
    for a in range(0, m_ref.shape[0], STEP):
        scores = m_ref[a : a + STEP, :] + row_ref[...]
        lse_ref[a // LANES : a // LANES + 1, :] = compact(row_lse_chunk(scores))


def column_kernel(log_mass, m_ref, own, mate, pair, lse_ref, f_ref, column_ref):
    potential = log_mass - combine(aligned([own[...], pair[0], mate[...], pair[1]]))
    f_ref[...] = potential
    put_column(column_ref, potential)
    columns = m_ref.shape[1]
    step = 32

    def fold(values, op):
        return functools.reduce(op, [values[b : b + 8] for b in range(0, step, 8)])

    highest = jnp.full((8, columns), -jnp.inf, jnp.float32)
    for a in range(0, m_ref.shape[0], step):
        highest = jnp.maximum(highest, fold(m_ref[a : a + step, :] + column_ref[a : a + step], jnp.maximum))
    highest = jnp.max(highest, axis=0, keepdims=True)
    total = jnp.zeros((8, columns), jnp.float32)
    for a in range(0, m_ref.shape[0], step):
        scores = m_ref[a : a + step, :] + column_ref[a : a + step]
        total = total + fold(jnp.exp2(scores - highest), jnp.add)
    lse = highest + jnp.log2(jnp.sum(total, axis=0, keepdims=True))
    for a in range(lse_ref.shape[0]):
        lse_ref[a : a + 1, :] = lse[:, a * LANES : (a + 1) * LANES]


def target_kernel(m_ref, x_ref, f, c, out_ref, column_ref, row_ref):
    put_column(column_ref, f[...])
    put_row(row_ref, c[...])
    step = 256
    for a in range(0, m_ref.shape[1], step):
        scores = m_ref[:, a : a + step] + column_ref[...]
        weights = jnp.exp2(scores - row_ref[:, a : a + step]).astype(jnp.bfloat16)
        out_ref[a : a + step, :] = lax.dot_general(
            weights, x_ref[...], (((0,), (0,)), ((), ())), preferred_element_type=jnp.float32
        ).astype(jnp.bfloat16)


def source_kernel(m_ref, y_ref, g, r, out_ref, column_ref, row_ref):
    put_row(row_ref, g[...])
    put_column(column_ref, r[...])
    for a in range(0, m_ref.shape[0], STEP):
        scores = m_ref[a : a + STEP, :] + row_ref[...]
        weights = jnp.exp2(scores - column_ref[a : a + STEP]).astype(jnp.bfloat16)
        out_ref[a : a + STEP, :] = jnp.dot(
            weights, y_ref[...], preferred_element_type=jnp.float32
        ).astype(jnp.bfloat16)


def join_kernel(p_ref, near_ref, own, mate, pair, out_ref, own_ref, mate_ref):
    half = out_ref.shape[0]
    parts = aligned([own[...], pair[0], mate[...], pair[1]])
    whole = combine(parts)
    top = whole.shape[0] // 2
    put_column(own_ref, jnp.exp2(parts[0] - whole)[:top])
    put_column(mate_ref, jnp.exp2(parts[2] - whole)[:top])
    mine = p_ref[0:half, :].astype(jnp.float32) * own_ref[...]
    out_ref[...] = (mine + near_ref[...].astype(jnp.float32) * mate_ref[...]).astype(jnp.bfloat16)


def finish_kernel(s_ref, far_ref, t_ref, t1, t2, t3, own, mate, pair, out_ref, c0, c1, c2, c3):
    rows = far_ref.shape[0]
    per = rows // 8
    summed = (s_ref[0:rows, :].astype(jnp.float32) + far_ref[...].astype(jnp.float32)).astype(jnp.bfloat16)
    parts = []
    for q, part in enumerate((own[...], mate[...], pair[0], pair[1])):
        lines = part.shape[0] // 4
        parts.append(part[q * lines : (q + 1) * lines])
    whole = combine(parts)
    pieces = [t_ref[0:rows, :], t1[...], t2[...], t3[...]]
    total = None
    for piece, part, column in zip(pieces, parts, (c0, c1, c2, c3)):
        put_column(column, jnp.exp2(part - whole))
        term = piece.astype(jnp.float32) * column[...]
        total = term if total is None else total + term
    total = total.astype(jnp.bfloat16)
    for k in range(8):
        out_ref[k, 0:per, :] = summed[k * per : (k + 1) * per]
        out_ref[k, per : 2 * per, :] = total[k * per : (k + 1) * per]


def shards(sources, targets, source_order, target_order):
    rows, width = sources.shape
    side = 4 * rows
    per = rows // 8
    log_mass = -math.log2(4 * side)
    scale = 1.0 / (width * entropy_weight * math.log(2.0))
    vmem = pl.BlockSpec(memory_space=pltpu.VMEM)
    f32, bf16 = jnp.float32, jnp.bfloat16
    tile = (side // LANES, LANES)
    area = side * side

    def out(shape, dtype):
        return jax.ShapeDtypeStruct(shape, dtype)

    def call(kernel, outs, scratch, args, flops=0, exps=0, aliases=None):
        return pl.pallas_call(
            kernel,
            out_shape=outs,
            in_specs=[vmem] * len(args),
            out_specs=[vmem] * len(outs),
            scratch_shapes=scratch,
            input_output_aliases=aliases or {},
            compiler_params=pltpu.CompilerParams(vmem_limit_bytes=VMEM_LIMIT),
            cost_estimate=pl.CostEstimate(flops=flops, bytes_accessed=4 * area, transcendentals=exps),
        )(*args)

    def column(n):
        return pltpu.VMEM((n, 1), f32)

    def line(n):
        return pltpu.VMEM((1, n), f32)

    flops = 2 * area * width
    source_line, target_line = source_order.reshape(1, rows), target_order.reshape(1, rows)
    (sent,) = call(
        pack_kernel, [out((8, 2 * per, width), bf16)], [], [source_line, sources, target_line, targets]
    )
    got = lax.all_to_all(sent, CLUSTER, split_axis=0, concat_axis=0, tiled=True)
    mine = got[:, :per].reshape(rows, width)
    aims = got[:, per:].reshape(rows, width)

    half = rows // 2
    s1 = lax.ppermute(mine, "zl", SWAP)
    t1 = lax.ppermute(aims, "y", NEXT)
    t2 = lax.ppermute(aims, "y", LAST)
    s2 = lax.ppermute(mine, "core", SWAP)
    s3 = lax.ppermute(s1, "core", SWAP)
    t3 = jnp.concatenate(
        [lax.ppermute(t2[:half], "y", NEXT), lax.ppermute(t1[half:], "y", LAST)], axis=0
    )
    matrix, all_sources, all_targets, part, norms = call(
        functools.partial(first_kernel, scale),
        [out((side, side), f32), out((side, width), bf16), out((side, width), bf16), out(tile, f32), out((side, 1), f32)],
        [line(3 * rows)],
        [mine, s1, s2, s3, aims, t1, t2],
        3 * flops // 4,
        area,
    )
    matrix, all_targets, row_part = call(
        functools.partial(second_kernel, scale),
        [out((side, side), f32), out((side, width), bf16), out(tile, f32)],
        [line(rows)],
        [all_sources, norms, part, t3, matrix, all_targets],
        flops // 4,
        area // 4,
        {4: 0, 5: 1},
    )

    def exchange_rows(value):
        mate = lax.ppermute(value, "core", SWAP)
        pair = lax.ppermute(jnp.stack([value, mate]), "zl", SWAP)
        return [value, mate, pair]

    def exchange_columns(value):
        mate = lax.ppermute(value, "y", NEXT)
        pair = lax.ppermute(jnp.stack([value, mate]), "y", LAST)
        return [value, mate, pair]

    for repeat in range(ITERS):
        column_part, source_potential = call(
            functools.partial(column_kernel, log_mass),
            [out(tile, f32), out(tile, f32)],
            [column(side)],
            [matrix] + exchange_rows(row_part),
            0,
            area,
        )
        column_parts = exchange_columns(column_part)
        row_part, target_potential = call(
            functools.partial(row_kernel, log_mass),
            [out(tile, f32), out(tile, f32)],
            [line(side)],
            [matrix] + column_parts,
            0,
            area,
        )

    (target_part,) = call(
        target_kernel,
        [out((side, width), bf16)],
        [column(side), line(side)],
        [matrix, all_sources, source_potential, column_part],
        flops,
        area,
    )
    target_pieces = [
        lax.ppermute(target_part[rows : 2 * rows], "y", NEXT),
        lax.ppermute(target_part[2 * rows : 3 * rows], "y", LAST),
        lax.ppermute(target_part[3 * rows :], "y", ACROSS),
    ]
    (source_part,) = call(
        source_kernel,
        [out((side, width), bf16)],
        [column(side), line(side)],
        [matrix, all_targets, target_potential, row_part],
        flops,
        area,
    )
    row_parts = exchange_rows(row_part)
    near = lax.ppermute(source_part[2 * rows :], "core", SWAP)
    (joined,) = call(
        join_kernel,
        [out((2 * rows, width), bf16)],
        [column(2 * rows)] * 2,
        [source_part, near] + row_parts,
    )
    far = lax.ppermute(joined[rows:], "zl", SWAP)
    (back,) = call(
        finish_kernel,
        [out((8, 2 * per, width), bf16)],
        [column(rows)] * 4,
        [joined, far, target_part] + target_pieces + column_parts,
    )
    back = lax.all_to_all(back, CLUSTER, split_axis=0, concat_axis=0, tiled=True)
    return call(
        unpack_kernel,
        [out((rows, width), bf16), out((rows, width), bf16)],
        [],
        [source_line, target_line, back],
    )


def solution(mesh):
    split = Mesh(mesh.devices.reshape(SIZES), AXES)
    return jax.shard_map(
        shards,
        mesh=split,
        in_specs=(P(AXES, None), P(AXES, None), P(AXES), P(AXES)),
        out_specs=(P(AXES, None), P(AXES, None)),
        check_vma=False,
    )
```

```python
import functools
import math

import jax
import jax.numpy as jnp
from jax import lax
from jax.experimental import pallas as pl
from jax.experimental.pallas import tpu as pltpu
from jax.sharding import Mesh, PartitionSpec as P


ITERS = 3
entropy_weight = 0.02
AXES = ("xh", "xl", "core", "zh", "zl", "yh", "yl")
SIZES = (2,) * 7
CLUSTER = ("xh", "zh", "yh")
SWAP = [(0, 1), (1, 0)]
ACROSS = [(i, i ^ 3) for i in range(4)]
VMEM_LIMIT = 24 * 1024 * 1024
LANES = 128
STEP = 128


def compact(column):
    rows = [
        jnp.transpose(jnp.broadcast_to(column[a : a + LANES], (LANES, LANES)))[0:1]
        for a in range(0, column.shape[0], LANES)
    ]
    return jnp.concatenate(rows, axis=0)


def combine(parts):
    highest = functools.reduce(jnp.maximum, parts)
    total = functools.reduce(jnp.add, [jnp.exp2(part - highest) for part in parts])
    return highest + jnp.log2(total)


def flip(part, q):
    per = part.shape[0] // 4
    return jnp.concatenate([part[(p ^ q) * per : ((p ^ q) + 1) * per] for p in range(4)], axis=0)


def aligned(parts):
    return [part if q == 0 else flip(part, q) for q, part in enumerate(parts)]


def put_row(row_ref, value):
    for a in range(value.shape[0]):
        row_ref[0:1, a * LANES : (a + 1) * LANES] = value[a : a + 1]


def put_column(column_ref, value):
    for a in range(value.shape[0]):
        spread = jnp.transpose(jnp.broadcast_to(value[a : a + 1], (LANES, LANES)))
        column_ref[a * LANES : (a + 1) * LANES] = spread[:, 0:1]


def row_lse_chunk(scores):
    highest = jnp.max(scores, axis=1, keepdims=True)
    total = jnp.sum(jnp.exp2(scores - highest), axis=1, keepdims=True)
    return highest + jnp.log2(total)


def pack_kernel(so_hbm, s_hbm, to_hbm, t_hbm, out_ref, so_ref, s_ref, to_ref, t_ref, sems):
    copies = [
        pltpu.make_async_copy(source, target, sems.at[n])
        for n, (source, target) in enumerate(
            ((so_hbm, so_ref), (s_hbm, s_ref), (to_hbm, to_ref), (t_hbm, t_ref))
        )
    ]
    for copy in copies:
        copy.start()
    rows = s_ref.shape[0]
    per = rows // 8
    slots = lax.broadcasted_iota(jnp.int32, (rows, rows), 0)
    for part, (order, matrix) in enumerate(((so_ref, s_ref), (to_ref, t_ref))):
        copies[2 * part].wait()
        copies[2 * part + 1].wait()
        chosen = jnp.where(slots == order[...], 1.0, 0.0).astype(jnp.bfloat16)
        moved = jnp.dot(chosen, matrix[...], preferred_element_type=jnp.float32).astype(jnp.bfloat16)
        for k in range(8):
            out_ref[k, part * per : (part + 1) * per, :] = moved[k * per : (k + 1) * per]


def unpack_kernel(so_ref, to_ref, back_ref, s_ref, t_ref):
    rows = s_ref.shape[0]
    per = rows // 8
    slots = lax.broadcasted_iota(jnp.int32, (rows, rows), 0)
    for part, (order, out) in enumerate(((so_ref, s_ref), (to_ref, t_ref))):
        chosen = jnp.where(slots == order[...], 1.0, 0.0).astype(jnp.bfloat16)
        moved = back_ref[:, part * per : (part + 1) * per, :].reshape(rows, out.shape[1])
        out[...] = lax.dot_general(
            chosen, moved, (((0,), (0,)), ((), ())), preferred_element_type=jnp.float32
        ).astype(jnp.bfloat16)


def target_norms(norm_ref, block, start):
    width = block.shape[1]
    for a in range(0, block.shape[0], LANES):
        wide = block[a : a + LANES, :].astype(jnp.float32)
        square = wide * wide
        folded = functools.reduce(jnp.add, [square[:, c : c + LANES] for c in range(0, width, LANES)])
        norm_ref[0:1, start + a : start + a + LANES] = jnp.sum(jnp.transpose(folded), axis=0, keepdims=True)


def score_block(scale, block, norms, targets, target_row):
    inner = lax.dot_general(block, targets, (((1,), (1,)), ((), ())), preferred_element_type=jnp.float32)
    return (2.0 * inner - norms - target_row) * scale


def first_kernel(scale, s0, s1, s2, s3, t0, t1, t2, m_ref, x_ref, y_ref, lse_ref, sn_ref, norm_ref):
    rows = s0.shape[0]
    for q, s in enumerate((s0, s1, s2, s3)):
        x_ref[q * rows : (q + 1) * rows, :] = s[...]
    for q, t in enumerate((t0, t1, t2)):
        y_ref[q * rows : (q + 1) * rows, :] = t[...]
        target_norms(norm_ref, t, q * rows)
    ready = 3 * rows
    for a in range(0, x_ref.shape[0], STEP):
        block = x_ref[a : a + STEP, :]
        wide = block.astype(jnp.float32)
        norms = jnp.sum(wide * wide, axis=1, keepdims=True)
        sn_ref[a : a + STEP] = norms
        scores = score_block(scale, block, norms, y_ref[0:ready, :], norm_ref[...])
        m_ref[a : a + STEP, 0:ready] = scores
        lse_ref[a // LANES : a // LANES + 1, :] = compact(row_lse_chunk(scores))


def second_kernel(scale, x_ref, sn_ref, part_ref, ta, tb, m_in, y_in, m_ref, y_ref, lse_ref, norm_ref):
    rows = 2 * ta.shape[0]
    ready = 3 * rows
    y_ref[ready : ready + rows // 2, :] = ta[...]
    y_ref[ready + rows // 2 : 4 * rows, :] = tb[...]
    t3 = y_ref.at[pl.ds(ready, rows)]
    target_norms(norm_ref, t3, 0)
    for a in range(0, x_ref.shape[0], STEP):
        scores = score_block(scale, x_ref[a : a + STEP, :], sn_ref[a : a + STEP], t3[...], norm_ref[...])
        m_ref[a : a + STEP, ready : 4 * rows] = scores
        g = a // LANES
        lse_ref[g : g + 1, :] = combine([part_ref[g : g + 1, :], compact(row_lse_chunk(scores))])


def row_kernel(log_mass, m_ref, own, mate, pair, lse_ref, g_ref, row_ref):
    potential = log_mass - combine(aligned([own[...], mate[...], pair[0], pair[1]]))
    g_ref[...] = potential
    put_row(row_ref, potential)
    for a in range(0, m_ref.shape[0], STEP):
        scores = m_ref[a : a + STEP, :] + row_ref[...]
        lse_ref[a // LANES : a // LANES + 1, :] = compact(row_lse_chunk(scores))


def column_kernel(log_mass, m_ref, own, mate, pair, lse_ref, f_ref, column_ref):
    potential = log_mass - combine(aligned([own[...], pair[0], mate[...], pair[1]]))
    f_ref[...] = potential
    put_column(column_ref, potential)
    columns = m_ref.shape[1]
    step = 32

    def fold(values, op):
        return functools.reduce(op, [values[b : b + 8] for b in range(0, step, 8)])

    highest = jnp.full((8, columns), -jnp.inf, jnp.float32)
    for a in range(0, m_ref.shape[0], step):
        highest = jnp.maximum(highest, fold(m_ref[a : a + step, :] + column_ref[a : a + step], jnp.maximum))
    highest = jnp.max(highest, axis=0, keepdims=True)
    total = jnp.zeros((8, columns), jnp.float32)
    for a in range(0, m_ref.shape[0], step):
        scores = m_ref[a : a + step, :] + column_ref[a : a + step]
        total = total + fold(jnp.exp2(scores - highest), jnp.add)
    lse = highest + jnp.log2(jnp.sum(total, axis=0, keepdims=True))
    for a in range(lse_ref.shape[0]):
        lse_ref[a : a + 1, :] = lse[:, a * LANES : (a + 1) * LANES]


def target_kernel(m_ref, x_ref, f, c, p1, p2, p3, p0, column_ref, row_ref):
    put_column(column_ref, f[...])
    put_row(row_ref, c[...])
    step = p0.shape[0]
    for a, out_ref in zip(range(0, m_ref.shape[1], step), (p0, p1, p2, p3)):
        scores = m_ref[:, a : a + step] + column_ref[...]
        weights = jnp.exp2(scores - row_ref[:, a : a + step]).astype(jnp.bfloat16)
        out_ref[...] = lax.dot_general(
            weights, x_ref[...], (((0,), (0,)), ((), ())), preferred_element_type=jnp.float32
        ).astype(jnp.bfloat16)


def source_kernel(m_ref, y_ref, g, r, near_ref, far_ref, column_ref, row_ref):
    put_row(row_ref, g[...])
    put_column(column_ref, r[...])
    half = near_ref.shape[0]
    for a in range(0, m_ref.shape[0], STEP):
        out_ref, b = (near_ref, a) if a < half else (far_ref, a - half)
        scores = m_ref[a : a + STEP, :] + row_ref[...]
        weights = jnp.exp2(scores - column_ref[a : a + STEP]).astype(jnp.bfloat16)
        out_ref[b : b + STEP, :] = jnp.dot(
            weights, y_ref[...], preferred_element_type=jnp.float32
        ).astype(jnp.bfloat16)


def join_kernel(p_ref, near_ref, own, mate, pair, out_ref, far_ref, own_ref, mate_ref):
    rows = out_ref.shape[0]
    parts = aligned([own[...], pair[0], mate[...], pair[1]])
    whole = combine(parts)
    top = whole.shape[0] // 2
    put_column(own_ref, jnp.exp2(parts[0] - whole)[:top])
    put_column(mate_ref, jnp.exp2(parts[2] - whole)[:top])
    mine = p_ref[...].astype(jnp.float32) * own_ref[...]
    joined = (mine + near_ref[...].astype(jnp.float32) * mate_ref[...]).astype(jnp.bfloat16)
    out_ref[...] = joined[:rows]
    far_ref[...] = joined[rows:]


def finish_kernel(s_ref, far_ref, t_ref, t1, t2, t3, own, mate, pair, out_ref, c0, c1, c2, c3):
    rows = far_ref.shape[0]
    per = rows // 8
    summed = (s_ref[...].astype(jnp.float32) + far_ref[...].astype(jnp.float32)).astype(jnp.bfloat16)
    parts = []
    for q, part in enumerate((own[...], mate[...], pair[0], pair[1])):
        lines = part.shape[0] // 4
        parts.append(part[q * lines : (q + 1) * lines])
    whole = combine(parts)
    pieces = [t_ref[...], t1[...], t2[...], t3[...]]
    total = None
    for piece, part, column in zip(pieces, parts, (c0, c1, c2, c3)):
        put_column(column, jnp.exp2(part - whole))
        term = piece.astype(jnp.float32) * column[...]
        total = term if total is None else total + term
    total = total.astype(jnp.bfloat16)
    for k in range(8):
        out_ref[k, 0:per, :] = summed[k * per : (k + 1) * per]
        out_ref[k, per : 2 * per, :] = total[k * per : (k + 1) * per]


def swap(value, axis, pairs=SWAP):
    return lax.ppermute(value, axis, pairs)


def whole(sources, targets, source_order, target_order):
    rows, width = sources.shape
    side = 4 * rows
    per = rows // 8
    log_mass = -math.log2(4 * side)
    scale = 1.0 / (width * entropy_weight * math.log(2.0))
    vmem = pl.BlockSpec(memory_space=pltpu.VMEM)
    hbm = pl.BlockSpec(memory_space=pltpu.HBM)
    f32, bf16 = jnp.float32, jnp.bfloat16
    tile = (side // LANES, LANES)
    area = side * side

    def out(shape, dtype):
        return jax.ShapeDtypeStruct(shape, dtype)

    def call(kernel, outs, scratch, args, flops=0, exps=0, aliases=None, spec=vmem, limit=VMEM_LIMIT):
        return pl.pallas_call(
            kernel,
            out_shape=outs,
            in_specs=[spec] * len(args),
            out_specs=[vmem] * len(outs),
            scratch_shapes=scratch,
            input_output_aliases=aliases or {},
            compiler_params=pltpu.CompilerParams(vmem_limit_bytes=limit),
            cost_estimate=pl.CostEstimate(flops=flops, bytes_accessed=4 * area, transcendentals=exps),
        )(*args)

    def column(n):
        return pltpu.VMEM((n, 1), f32)

    def line(n):
        return pltpu.VMEM((1, n), f32)

    flops = 2 * area * width
    source_line, target_line = source_order.reshape(1, rows), target_order.reshape(1, rows)
    order_block, row_block = pltpu.VMEM((1, rows), jnp.int32), pltpu.VMEM((rows, width), bf16)
    (sent,) = call(
        pack_kernel,
        [out((8, 2 * per, width), bf16)],
        [order_block, row_block, order_block, row_block, pltpu.SemaphoreType.DMA((4,))],
        [source_line, sources, target_line, targets],
        spec=hbm,
        limit=60 * 1024 * 1024,
    )
    got = lax.all_to_all(sent, CLUSTER, split_axis=0, concat_axis=0, tiled=True)
    mine = got[:, :per].reshape(rows, width)
    aims = got[:, per:].reshape(rows, width)

    half = rows // 2
    t1 = swap(aims, "yl")
    t2 = swap(aims, "xl")
    s1 = swap(mine, "zl")
    s2 = swap(mine, "core")
    s3 = swap(s1, "core")
    t3a = swap(t2[:half], "yl")
    t3b = swap(t1[half:], "xl")
    matrix, all_sources, all_targets, part, norms = call(
        functools.partial(first_kernel, scale),
        [out((side, side), f32), out((side, width), bf16), out((side, width), bf16), out(tile, f32), out((side, 1), f32)],
        [line(3 * rows)],
        [mine, s1, s2, s3, aims, t1, t2],
        3 * flops // 4,
        area,
    )
    matrix, all_targets, row_part = call(
        functools.partial(second_kernel, scale),
        [out((side, side), f32), out((side, width), bf16), out(tile, f32)],
        [line(rows)],
        [all_sources, norms, part, t3a, t3b, matrix, all_targets],
        flops // 4,
        area // 4,
        {5: 0, 6: 1},
    )

    def exchange_rows(value):
        mate = swap(value, "core")
        pair = swap(jnp.stack([value, mate]), "zl")
        return [value, mate, pair]

    def exchange_columns(value):
        mate = swap(value, "yl")
        pair = swap(jnp.stack([value, mate]), "xl")
        return [value, mate, pair]

    for _ in range(ITERS):
        column_part, source_potential = call(
            functools.partial(column_kernel, log_mass),
            [out(tile, f32), out(tile, f32)],
            [column(side)],
            [matrix] + exchange_rows(row_part),
            0,
            area,
        )
        column_parts = exchange_columns(column_part)
        row_part, target_potential = call(
            functools.partial(row_kernel, log_mass),
            [out(tile, f32), out(tile, f32)],
            [line(side)],
            [matrix] + column_parts,
            0,
            area,
        )

    piece_1, piece_2, piece_3, own_piece = call(
        target_kernel,
        [out((rows, width), bf16)] * 4,
        [column(side), line(side)],
        [matrix, all_sources, source_potential, column_part],
        flops,
        area,
    )
    target_pieces = [own_piece, swap(piece_1, "yl"), swap(piece_2, "xl"), swap(piece_3, ("xl", "yl"), ACROSS)]
    source_near, source_far = call(
        source_kernel,
        [out((2 * rows, width), bf16), out((2 * rows, width), bf16)],
        [column(side), line(side)],
        [matrix, all_targets, target_potential, row_part],
        flops,
        area,
    )
    row_parts = exchange_rows(row_part)
    near = swap(source_far, "core")
    joined_own, joined_far = call(
        join_kernel,
        [out((rows, width), bf16), out((rows, width), bf16)],
        [column(2 * rows)] * 2,
        [source_near, near] + row_parts,
    )
    far = swap(joined_far, "zl")
    (back,) = call(
        finish_kernel,
        [out((8, 2 * per, width), bf16)],
        [column(rows)] * 4,
        [joined_own, far] + target_pieces + column_parts,
    )
    back = lax.all_to_all(back, CLUSTER, split_axis=0, concat_axis=0, tiled=True)
    return call(
        unpack_kernel, [out((rows, width), bf16), out((rows, width), bf16)], [], [source_line, target_line, back]
    )


def solution(mesh):
    split = Mesh(mesh.devices.reshape(SIZES), AXES)
    return jax.shard_map(
        whole,
        mesh=split,
        in_specs=(P(AXES, None), P(AXES, None), P(AXES), P(AXES)),
        out_specs=(P(AXES, None), P(AXES, None)),
        check_vma=False,
    )
```

```python
import functools
import itertools
import math

import jax
import jax.numpy as jnp
from jax import lax
from jax.experimental import pallas as pl
from jax.experimental.pallas import tpu as pltpu
from jax.sharding import Mesh, PartitionSpec as P


ITERS = 3
entropy_weight = 0.02
AXES = ("xh", "xl", "core", "zh", "zl", "yh", "yl")
SIZES = (2,) * 7
SWAP = [(0, 1), (1, 0)]
ACROSS = [(i, i ^ 3) for i in range(4)]
VMEM_LIMIT = 24 * 1024 * 1024
LANES = 128
STEP = 128


def compact(column):
    rows = [
        jnp.transpose(jnp.broadcast_to(column[a : a + LANES], (LANES, LANES)))[0:1]
        for a in range(0, column.shape[0], LANES)
    ]
    return jnp.concatenate(rows, axis=0)


def combine(parts):
    highest = functools.reduce(jnp.maximum, parts)
    total = functools.reduce(jnp.add, [jnp.exp2(part - highest) for part in parts])
    return highest + jnp.log2(total)


def flip(part, q):
    per = part.shape[0] // 4
    return jnp.concatenate([part[(p ^ q) * per : ((p ^ q) + 1) * per] for p in range(4)], axis=0)


def aligned(parts):
    return [part if q == 0 else flip(part, q) for q, part in enumerate(parts)]


def put_row(row_ref, value):
    for a in range(value.shape[0]):
        row_ref[0:1, a * LANES : (a + 1) * LANES] = value[a : a + 1]


def put_column(column_ref, value):
    for a in range(value.shape[0]):
        spread = jnp.transpose(jnp.broadcast_to(value[a : a + 1], (LANES, LANES)))
        column_ref[a * LANES : (a + 1) * LANES] = spread[:, 0:1]


def row_lse_chunk(scores):
    highest = jnp.max(scores, axis=1, keepdims=True)
    total = jnp.sum(jnp.exp2(scores - highest), axis=1, keepdims=True)
    return highest + jnp.log2(total)


def pack_kernel(so_hbm, s_hbm, to_hbm, t_hbm, out_ref, so_ref, s_ref, to_ref, t_ref, sems):
    copies = [
        pltpu.make_async_copy(source, target, sems.at[n])
        for n, (source, target) in enumerate(
            ((so_hbm, so_ref), (s_hbm, s_ref), (to_hbm, to_ref), (t_hbm, t_ref))
        )
    ]
    for copy in copies:
        copy.start()
    rows = s_ref.shape[0]
    per = rows // 8
    slots = lax.broadcasted_iota(jnp.int32, (rows, rows), 0)
    for part, (order, matrix) in enumerate(((so_ref, s_ref), (to_ref, t_ref))):
        copies[2 * part].wait()
        copies[2 * part + 1].wait()
        chosen = jnp.where(slots == order[...], 1.0, 0.0).astype(jnp.bfloat16)
        moved = jnp.dot(chosen, matrix[...], preferred_element_type=jnp.float32).astype(jnp.bfloat16)
        for k in range(8):
            out_ref[k, part * per : (part + 1) * per, :] = moved[k * per : (k + 1) * per]


def unpack_kernel(so_ref, to_ref, back_ref, s_ref, t_ref):
    rows = s_ref.shape[0]
    per = rows // 8
    slots = lax.broadcasted_iota(jnp.int32, (rows, rows), 0)
    for part, (order, out) in enumerate(((so_ref, s_ref), (to_ref, t_ref))):
        chosen = jnp.where(slots == order[...], 1.0, 0.0).astype(jnp.bfloat16)
        moved = back_ref[:, part * per : (part + 1) * per, :].reshape(rows, out.shape[1])
        out[...] = lax.dot_general(
            chosen, moved, (((0,), (0,)), ((), ())), preferred_element_type=jnp.float32
        ).astype(jnp.bfloat16)


def target_norms(norm_ref, block, start):
    width = block.shape[1]
    for a in range(0, block.shape[0], LANES):
        wide = block[a : a + LANES, :].astype(jnp.float32)
        square = wide * wide
        folded = functools.reduce(jnp.add, [square[:, c : c + LANES] for c in range(0, width, LANES)])
        norm_ref[0:1, start + a : start + a + LANES] = jnp.sum(jnp.transpose(folded), axis=0, keepdims=True)


def score_rows(scale, rows, x_ref, y_ref, line_ref, m_ref, lse_ref):
    for a in rows:
        block = x_ref[a : a + STEP, :]
        wide = block.astype(jnp.float32)
        norms = jnp.sum(wide * wide, axis=1, keepdims=True)
        inner = lax.dot_general(block, y_ref[...], (((1,), (1,)), ((), ())), preferred_element_type=jnp.float32)
        scores = (2.0 * inner - norms - line_ref[...]) * scale
        m_ref[a : a + STEP, :] = scores
        lse_ref[a // LANES : a // LANES + 1, :] = compact(row_lse_chunk(scores))


def first_kernel(scale, s0, s1, s2, t0, t1, t2, t3, m_ref, x_ref, y_ref, lse_ref, line_ref):
    rows = s0.shape[0]
    for q, s in enumerate((s0, s1, s2)):
        x_ref[q * rows : (q + 1) * rows, :] = s[...]
    for q, t in enumerate((t0, t1, t2, t3)):
        y_ref[q * rows : (q + 1) * rows, :] = t[...]
        target_norms(line_ref, t, q * rows)
    score_rows(scale, range(0, 3 * rows, STEP), x_ref, y_ref, line_ref, m_ref, lse_ref)


def second_kernel(scale, y_ref, line_ref, part_ref, sa, sb, m_in, x_in, m_ref, x_ref, lse_ref):
    half = sa.shape[0]
    ready = 6 * half
    x_ref[ready : ready + half, :] = sa[...]
    x_ref[ready + half : ready + 2 * half, :] = sb[...]
    lines = ready // LANES
    lse_ref[0:lines, :] = part_ref[0:lines, :]
    score_rows(scale, range(ready, ready + 2 * half, STEP), x_ref, y_ref, line_ref, m_ref, lse_ref)


def row_kernel(log_mass, m_ref, c0, c1, c2, c3, lse_ref, row_ref):
    put_row(row_ref, log_mass - combine(aligned([c0[...], c1[...], c2[...], c3[...]])))
    for a in range(0, m_ref.shape[0], STEP):
        scores = m_ref[a : a + STEP, :] + row_ref[...]
        lse_ref[a // LANES : a // LANES + 1, :] = compact(row_lse_chunk(scores))


def column_kernel(log_mass, m_ref, r0, r1, r2, r3, lse_ref, f_ref, column_ref):
    potential = log_mass - combine(aligned([r0[...], r1[...], r2[...], r3[...]]))
    f_ref[...] = potential
    put_column(column_ref, potential)
    columns = m_ref.shape[1]
    step = 32

    def fold(values, op):
        return functools.reduce(op, [values[b : b + 8] for b in range(0, step, 8)])

    highest = jnp.full((8, columns), -jnp.inf, jnp.float32)
    for a in range(0, m_ref.shape[0], step):
        highest = jnp.maximum(highest, fold(m_ref[a : a + step, :] + column_ref[a : a + step], jnp.maximum))
    highest = jnp.max(highest, axis=0, keepdims=True)
    total = jnp.zeros((8, columns), jnp.float32)
    for a in range(0, m_ref.shape[0], step):
        scores = m_ref[a : a + step, :] + column_ref[a : a + step]
        total = total + fold(jnp.exp2(scores - highest), jnp.add)
    lse = highest + jnp.log2(jnp.sum(total, axis=0, keepdims=True))
    for a in range(lse_ref.shape[0]):
        lse_ref[a : a + 1, :] = lse[:, a * LANES : (a + 1) * LANES]


def target_kernel(m_ref, x_ref, f, c, near_ref, far_ref, column_ref, row_ref):
    put_column(column_ref, f[...])
    put_row(row_ref, c[...])
    step = 256
    half = near_ref.shape[0]
    for a in range(0, m_ref.shape[1], step):
        out_ref, b = (near_ref, a) if a < half else (far_ref, a - half)
        scores = m_ref[:, a : a + step] + column_ref[...]
        weights = jnp.exp2(scores - row_ref[:, a : a + step]).astype(jnp.bfloat16)
        out_ref[b : b + step, :] = lax.dot_general(
            weights, x_ref[...], (((0,), (0,)), ((), ())), preferred_element_type=jnp.float32
        ).astype(jnp.bfloat16)


def source_kernel(log_mass, m_ref, y_ref, c0, c1, c2, c3, p0, p1, p2, p3, lse_ref, row_ref):
    put_row(row_ref, log_mass - combine(aligned([c0[...], c1[...], c2[...], c3[...]])))
    rows = p0.shape[0]
    for a in range(0, m_ref.shape[0], STEP):
        scores = m_ref[a : a + STEP, :] + row_ref[...]
        highest = jnp.max(scores, axis=1, keepdims=True)
        raised = jnp.exp2(scores - highest)
        total = jnp.sum(raised, axis=1, keepdims=True)
        mapped = jnp.dot(raised.astype(jnp.bfloat16), y_ref[...], preferred_element_type=jnp.float32)
        out_ref, b = (p0, p1, p2, p3)[a // rows], a % rows
        out_ref[b : b + STEP, :] = (mapped / total).astype(jnp.bfloat16)
        lse_ref[a // LANES : a // LANES + 1, :] = compact(highest + jnp.log2(total))


def join_kernel(p_ref, near_ref, c0, c1, c2, c3, out_ref, far_ref, own_ref, mate_ref):
    rows = out_ref.shape[0]
    parts = aligned([c0[...], c1[...], c2[...], c3[...]])
    whole = combine(parts)
    top = whole.shape[0] // 2
    put_column(own_ref, jnp.exp2(parts[0] - whole)[:top])
    put_column(mate_ref, jnp.exp2(parts[2] - whole)[:top])
    mine = p_ref[...].astype(jnp.float32) * own_ref[...]
    joined = (mine + near_ref[...].astype(jnp.float32) * mate_ref[...]).astype(jnp.bfloat16)
    out_ref[...] = joined[:rows]
    far_ref[...] = joined[rows:]


def finish_kernel(t_ref, far_ref, s0, s1, s2, s3, r0, r1, r2, r3, out_ref, w0, w1, w2, w3):
    rows = t_ref.shape[0]
    per = rows // 8
    parts = []
    for q, part in enumerate((r0, r1, r2, r3)):
        lines = part.shape[0] // 4
        parts.append(part[q * lines : (q + 1) * lines, :])
    whole = combine(parts)
    total = None
    for piece, part, column in zip((s0, s1, s2, s3), parts, (w0, w1, w2, w3)):
        put_column(column, jnp.exp2(part - whole))
        term = piece[...].astype(jnp.float32) * column[...]
        total = term if total is None else total + term
    total = total.astype(jnp.bfloat16)
    summed = (t_ref[...].astype(jnp.float32) + far_ref[...].astype(jnp.float32)).astype(jnp.bfloat16)
    for k in range(8):
        out_ref[k, 0:per, :] = total[k * per : (k + 1) * per]
        out_ref[k, per : 2 * per, :] = summed[k * per : (k + 1) * per]


def swap(value, axis, pairs=SWAP):
    return lax.ppermute(value, axis, pairs)


def place_of(xh, xl, core, zh, zl, yh, yl):
    index = 0
    for bit in (xh, xl, core, zh, zl, yh, yl):
        index = 2 * index + bit
    return index


def groups():
    return [
        [
            place_of(xh, gx ^ xh, core, zh, gz ^ zh, yh, gy ^ yh)
            for xh, zh, yh in itertools.product((0, 1), repeat=3)
        ]
        for gx, core, gz, gy in itertools.product((0, 1), repeat=4)
    ]


def across(value):
    return lax.all_to_all(value, AXES, split_axis=0, concat_axis=0, axis_index_groups=groups(), tiled=True)


def whole(sources, targets, source_order, target_order):
    rows, width = sources.shape
    side = 4 * rows
    per = rows // 8
    log_mass = -math.log2(4 * side)
    scale = 1.0 / (width * entropy_weight * math.log(2.0))
    vmem = pl.BlockSpec(memory_space=pltpu.VMEM)
    hbm = pl.BlockSpec(memory_space=pltpu.HBM)
    f32, bf16 = jnp.float32, jnp.bfloat16
    tile = (side // LANES, LANES)
    area = side * side

    def out(shape, dtype):
        return jax.ShapeDtypeStruct(shape, dtype)

    def call(kernel, outs, scratch, args, flops=0, exps=0, aliases=None, spec=vmem, limit=VMEM_LIMIT):
        return pl.pallas_call(
            kernel,
            out_shape=outs,
            in_specs=[spec] * len(args),
            out_specs=[vmem] * len(outs),
            scratch_shapes=scratch,
            input_output_aliases=aliases or {},
            compiler_params=pltpu.CompilerParams(vmem_limit_bytes=limit),
            cost_estimate=pl.CostEstimate(flops=flops, bytes_accessed=4 * area, transcendentals=exps),
        )(*args)

    def column(n):
        return pltpu.VMEM((n, 1), f32)

    def line(n):
        return pltpu.VMEM((1, n), f32)

    flops = 2 * area * width
    source_line, target_line = source_order.reshape(1, rows), target_order.reshape(1, rows)
    order_block, row_block = pltpu.VMEM((1, rows), jnp.int32), pltpu.VMEM((rows, width), bf16)
    (sent,) = call(
        pack_kernel,
        [out((8, 2 * per, width), bf16)],
        [order_block, row_block, order_block, row_block, pltpu.SemaphoreType.DMA((4,))],
        [source_line, sources, target_line, targets],
        spec=hbm,
        limit=60 * 1024 * 1024,
    )
    got = across(sent)
    mine = got[:, :per].reshape(rows, width)
    aims = got[:, per:].reshape(rows, width)

    half = rows // 2
    s1 = swap(mine, "yl")
    s2 = swap(mine, "xl")
    t1 = swap(aims, "zl")
    t2 = swap(aims, "core")
    t3 = swap(t1, "core")
    s3a = swap(s2[:half], "yl")
    s3b = swap(s1[half:], "xl")
    matrix, all_sources, all_targets, part, norms = call(
        functools.partial(first_kernel, scale),
        [out((side, side), f32), out((side, width), bf16), out((side, width), bf16), out(tile, f32), out((1, side), f32)],
        [],
        [mine, s1, s2, aims, t1, t2, t3],
        3 * flops // 4,
        area,
    )
    matrix, all_sources, row_part = call(
        functools.partial(second_kernel, scale),
        [out((side, side), f32), out((side, width), bf16), out(tile, f32)],
        [],
        [all_targets, norms, part, s3a, s3b, matrix, all_sources],
        flops // 4,
        area // 4,
        {5: 0, 6: 1},
    )

    def exchange(value, slow, fast):
        both = swap(value, (slow, fast), ACROSS)
        second = swap(value, slow)
        first = swap(value, fast)
        return [value, first, second, both]

    for repeat in range(ITERS):
        column_part, source_potential = call(
            functools.partial(column_kernel, log_mass),
            [out(tile, f32), out(tile, f32)],
            [column(side)],
            [matrix] + exchange(row_part, "xl", "yl"),
            0,
            area,
        )
        column_parts = exchange(column_part, "core", "zl")
        if repeat < ITERS - 1:
            (row_part,) = call(
                functools.partial(row_kernel, log_mass),
                [out(tile, f32)],
                [line(side)],
                [matrix] + column_parts,
                0,
                area,
            )

    target_near, target_far = call(
        target_kernel,
        [out((2 * rows, width), bf16)] * 2,
        [column(side), line(side)],
        [matrix, all_sources, source_potential, column_part],
        flops,
        area,
    )
    near = swap(target_far, "core")
    own_piece, piece_1, piece_2, piece_3, row_part = call(
        functools.partial(source_kernel, log_mass),
        [out((rows, width), bf16)] * 4 + [out(tile, f32)],
        [line(side)],
        [matrix, all_targets] + column_parts,
        flops,
        area,
    )
    source_pieces = [own_piece, swap(piece_1, "yl"), swap(piece_2, "xl"), swap(piece_3, ("xl", "yl"), ACROSS)]
    row_parts = exchange(row_part, "xl", "yl")
    joined_own, joined_far = call(
        join_kernel, [out((rows, width), bf16)] * 2, [column(2 * rows)] * 2, [target_near, near] + column_parts
    )
    far = swap(joined_far, "zl")
    (back,) = call(
        finish_kernel,
        [out((8, 2 * per, width), bf16)],
        [column(rows)] * 4,
        [joined_own, far] + source_pieces + row_parts,
    )
    return call(
        unpack_kernel,
        [out((rows, width), bf16), out((rows, width), bf16)],
        [],
        [source_line, target_line, across(back)],
    )


def solution(mesh):
    split = Mesh(mesh.devices.reshape(SIZES), AXES)
    return jax.shard_map(
        whole,
        mesh=split,
        in_specs=(P(AXES, None), P(AXES, None), P(AXES), P(AXES)),
        out_specs=(P(AXES, None), P(AXES, None)),
        check_vma=False,
    )
```

```python
import functools
import itertools
import math

import jax
import jax.numpy as jnp
from jax import lax
from jax.experimental import pallas as pl
from jax.experimental.pallas import tpu as pltpu
from jax.sharding import Mesh, PartitionSpec as P


ITERS = 3
entropy_weight = 0.02
AXES = ("xh", "xl", "core", "zh", "zl", "yh", "yl")
SIZES = (2,) * 7
SWAP = [(0, 1), (1, 0)]
ACROSS = [(i, i ^ 3) for i in range(4)]
VMEM_LIMIT = 24 * 1024 * 1024
LANES = 128
STEP = 128
SPLIT = ((3,), (1, 2, 0))


def compact(column):
    rows = [
        jnp.transpose(jnp.broadcast_to(column[a : a + LANES], (LANES, LANES)))[0:1]
        for a in range(0, column.shape[0], LANES)
    ]
    return jnp.concatenate(rows, axis=0)


def combine(parts):
    highest = functools.reduce(jnp.maximum, parts)
    total = functools.reduce(jnp.add, [jnp.exp2(part - highest) for part in parts])
    return highest + jnp.log2(total)


def flip(part, q):
    per = part.shape[0] // 4
    return jnp.concatenate([part[(p ^ q) * per : ((p ^ q) + 1) * per] for p in range(4)], axis=0)


def aligned(parts):
    return [part if q == 0 else flip(part, q) for q, part in enumerate(parts)]


def put_row(row_ref, value):
    for a in range(value.shape[0]):
        row_ref[0:1, a * LANES : (a + 1) * LANES] = value[a : a + 1]


def put_column(column_ref, value):
    for a in range(value.shape[0]):
        spread = jnp.transpose(jnp.broadcast_to(value[a : a + 1], (LANES, LANES)))
        column_ref[a * LANES : (a + 1) * LANES] = spread[:, 0:1]


def row_lse_chunk(scores):
    highest = jnp.max(scores, axis=1, keepdims=True)
    total = jnp.sum(jnp.exp2(scores - highest), axis=1, keepdims=True)
    return highest + jnp.log2(total)


def pack_kernel(so_hbm, s_hbm, to_hbm, t_hbm, out_ref, so_ref, s_ref, to_ref, t_ref, sems):
    copies = [
        pltpu.make_async_copy(source, target, sems.at[n])
        for n, (source, target) in enumerate(
            ((so_hbm, so_ref), (s_hbm, s_ref), (to_hbm, to_ref), (t_hbm, t_ref))
        )
    ]
    for copy in copies:
        copy.start()
    rows = s_ref.shape[0]
    per = rows // 8
    slots = lax.broadcasted_iota(jnp.int32, (rows, rows), 0)
    for part, (order, matrix) in enumerate(((so_ref, s_ref), (to_ref, t_ref))):
        copies[2 * part].wait()
        copies[2 * part + 1].wait()
        chosen = jnp.where(slots == order[...], 1.0, 0.0).astype(jnp.bfloat16)
        moved = jnp.dot(chosen, matrix[...], preferred_element_type=jnp.float32).astype(jnp.bfloat16)
        for k in range(8):
            out_ref[k, part * per : (part + 1) * per, :] = moved[k * per : (k + 1) * per]


def unpack_kernel(so_ref, to_ref, back_ref, s_ref, t_ref):
    rows = s_ref.shape[0]
    per = rows // 8
    slots = lax.broadcasted_iota(jnp.int32, (rows, rows), 0)
    for part, (order, out) in enumerate(((so_ref, s_ref), (to_ref, t_ref))):
        chosen = jnp.where(slots == order[...], 1.0, 0.0).astype(jnp.bfloat16)
        moved = back_ref[:, part * per : (part + 1) * per, :].reshape(rows, out.shape[1])
        out[...] = lax.dot_general(
            chosen, moved, (((0,), (0,)), ((), ())), preferred_element_type=jnp.float32
        ).astype(jnp.bfloat16)


def target_norms(norm_ref, block, start):
    width = block.shape[1]
    for a in range(0, block.shape[0], LANES):
        wide = block[a : a + LANES, :].astype(jnp.float32)
        square = wide * wide
        folded = functools.reduce(jnp.add, [square[:, c : c + LANES] for c in range(0, width, LANES)])
        norm_ref[0:1, start + a : start + a + LANES] = jnp.sum(jnp.transpose(folded), axis=0, keepdims=True)


def score_rows(scale, rows, x_ref, y_ref, line_ref, m_ref, lse_ref):
    for a in rows:
        block = x_ref[a : a + STEP, :]
        wide = block.astype(jnp.float32)
        norms = jnp.sum(wide * wide, axis=1, keepdims=True)
        inner = lax.dot_general(block, y_ref[...], (((1,), (1,)), ((), ())), preferred_element_type=jnp.float32)
        scores = (2.0 * inner - norms - line_ref[...]) * scale
        m_ref[a : a + STEP, :] = scores
        lse_ref[a // LANES : a // LANES + 1, :] = compact(row_lse_chunk(scores))


def first_kernel(scale, s0, s1, s2, t0, t1, t2, t3, m_ref, x_ref, y_ref, lse_ref, line_ref):
    rows = s0.shape[0]
    for q, s in enumerate((s0, s1, s2)):
        x_ref[q * rows : (q + 1) * rows, :] = s[...]
    for q, t in enumerate((t0, t1, t2, t3)):
        y_ref[q * rows : (q + 1) * rows, :] = t[...]
        target_norms(line_ref, t, q * rows)
    score_rows(scale, range(0, 3 * rows, STEP), x_ref, y_ref, line_ref, m_ref, lse_ref)


def second_kernel(scale, y_ref, line_ref, part_ref, sa, sb, m_in, x_in, m_ref, x_ref, lse_ref):
    half = sa.shape[0]
    ready = 6 * half
    x_ref[ready : ready + half, :] = sa[...]
    x_ref[ready + half : ready + 2 * half, :] = sb[...]
    lines = ready // LANES
    lse_ref[0:lines, :] = part_ref[0:lines, :]
    score_rows(scale, range(ready, ready + 2 * half, STEP), x_ref, y_ref, line_ref, m_ref, lse_ref)


def row_kernel(log_mass, m_ref, c0, c1, c2, c3, lse_ref, row_ref):
    put_row(row_ref, log_mass - combine(aligned([c0[...], c1[...], c2[...], c3[...]])))
    for a in range(0, m_ref.shape[0], STEP):
        scores = m_ref[a : a + STEP, :] + row_ref[...]
        lse_ref[a // LANES : a // LANES + 1, :] = compact(row_lse_chunk(scores))


def column_kernel(log_mass, m_ref, r0, r1, r2, r3, lse_ref, f_ref, column_ref):
    potential = log_mass - combine(aligned([r0[...], r1[...], r2[...], r3[...]]))
    f_ref[...] = potential
    put_column(column_ref, potential)
    columns = m_ref.shape[1]
    step = 32

    def fold(values, op):
        return functools.reduce(op, [values[b : b + 8] for b in range(0, step, 8)])

    highest = jnp.full((8, columns), -jnp.inf, jnp.float32)
    for a in range(0, m_ref.shape[0], step):
        highest = jnp.maximum(highest, fold(m_ref[a : a + step, :] + column_ref[a : a + step], jnp.maximum))
    highest = jnp.max(highest, axis=0, keepdims=True)
    total = jnp.zeros((8, columns), jnp.float32)
    for a in range(0, m_ref.shape[0], step):
        scores = m_ref[a : a + step, :] + column_ref[a : a + step]
        total = total + fold(jnp.exp2(scores - highest), jnp.add)
    lse = highest + jnp.log2(jnp.sum(total, axis=0, keepdims=True))
    for a in range(lse_ref.shape[0]):
        lse_ref[a : a + 1, :] = lse[:, a * LANES : (a + 1) * LANES]


def target_kernel(m_ref, x_ref, f, c, near_ref, far_ref, column_ref, row_ref):
    put_column(column_ref, f[...])
    put_row(row_ref, c[...])
    step = 256
    half = near_ref.shape[0]
    for a in range(0, m_ref.shape[1], step):
        out_ref, b = (near_ref, a) if a < half else (far_ref, a - half)
        scores = m_ref[:, a : a + step] + column_ref[...]
        weights = jnp.exp2(scores - row_ref[:, a : a + step]).astype(jnp.bfloat16)
        out_ref[b : b + step, :] = lax.dot_general(
            weights, x_ref[...], (((0,), (0,)), ((), ())), preferred_element_type=jnp.float32
        ).astype(jnp.bfloat16)


def source_kernel(log_mass, blocks, m_ref, y_ref, c0, c1, c2, c3, *refs):
    *pieces, lse_ref, row_ref = refs
    put_row(row_ref, log_mass - combine(aligned([c0[...], c1[...], c2[...], c3[...]])))
    rows = pieces[0].shape[0]
    for place, a in enumerate(a for q in blocks for a in range(q * rows, (q + 1) * rows, STEP)):
        scores = m_ref[a : a + STEP, :] + row_ref[...]
        highest = jnp.max(scores, axis=1, keepdims=True)
        raised = jnp.exp2(scores - highest)
        total = jnp.sum(raised, axis=1, keepdims=True)
        mapped = jnp.dot(raised.astype(jnp.bfloat16), y_ref[...], preferred_element_type=jnp.float32)
        pieces[place * STEP // rows][a % rows : a % rows + STEP, :] = (mapped / total).astype(jnp.bfloat16)
        lse_ref[place : place + 1, :] = compact(highest + jnp.log2(total))


def join_kernel(p_ref, near_ref, c0, c1, c2, c3, out_ref, far_ref, own_ref, mate_ref):
    rows = out_ref.shape[0]
    parts = aligned([c0[...], c1[...], c2[...], c3[...]])
    whole = combine(parts)
    top = whole.shape[0] // 2
    put_column(own_ref, jnp.exp2(parts[0] - whole)[:top])
    put_column(mate_ref, jnp.exp2(parts[2] - whole)[:top])
    mine = p_ref[...].astype(jnp.float32) * own_ref[...]
    joined = (mine + near_ref[...].astype(jnp.float32) * mate_ref[...]).astype(jnp.bfloat16)
    out_ref[...] = joined[:rows]
    far_ref[...] = joined[rows:]


def finish_kernel(t_ref, far_ref, s0, s1, s2, s3, r0, r1, r2, r3, out_ref, w0, w1, w2, w3):
    rows = t_ref.shape[0]
    per = rows // 8
    parts = []
    for q, part in enumerate((r0, r1, r2, r3)):
        lines = part.shape[0] // 4
        parts.append(part[q * lines : (q + 1) * lines, :])
    whole = combine(parts)
    total = None
    for piece, part, column in zip((s0, s1, s2, s3), parts, (w0, w1, w2, w3)):
        put_column(column, jnp.exp2(part - whole))
        term = piece[...].astype(jnp.float32) * column[...]
        total = term if total is None else total + term
    total = total.astype(jnp.bfloat16)
    summed = (t_ref[...].astype(jnp.float32) + far_ref[...].astype(jnp.float32)).astype(jnp.bfloat16)
    for k in range(8):
        out_ref[k, 0:per, :] = total[k * per : (k + 1) * per]
        out_ref[k, per : 2 * per, :] = summed[k * per : (k + 1) * per]


def swap(value, axis, pairs=SWAP):
    return lax.ppermute(value, axis, pairs)


def place_of(xh, xl, core, zh, zl, yh, yl):
    index = 0
    for bit in (xh, xl, core, zh, zl, yh, yl):
        index = 2 * index + bit
    return index


def groups():
    return [
        [
            place_of(xh, gx ^ xh, core, zh, gz ^ zh, yh, gy ^ yh)
            for xh, zh, yh in itertools.product((0, 1), repeat=3)
        ]
        for gx, core, gz, gy in itertools.product((0, 1), repeat=4)
    ]


def across(value):
    return lax.all_to_all(value, AXES, split_axis=0, concat_axis=0, axis_index_groups=groups(), tiled=True)


def whole(sources, targets, source_order, target_order):
    rows, width = sources.shape
    side = 4 * rows
    per = rows // 8
    log_mass = -math.log2(4 * side)
    scale = 1.0 / (width * entropy_weight * math.log(2.0))
    vmem = pl.BlockSpec(memory_space=pltpu.VMEM)
    hbm = pl.BlockSpec(memory_space=pltpu.HBM)
    f32, bf16 = jnp.float32, jnp.bfloat16
    tile = (side // LANES, LANES)
    area = side * side

    def out(shape, dtype):
        return jax.ShapeDtypeStruct(shape, dtype)

    def call(kernel, outs, scratch, args, flops=0, exps=0, aliases=None, spec=vmem, limit=VMEM_LIMIT):
        return pl.pallas_call(
            kernel,
            out_shape=outs,
            in_specs=[spec] * len(args),
            out_specs=[vmem] * len(outs),
            scratch_shapes=scratch,
            input_output_aliases=aliases or {},
            compiler_params=pltpu.CompilerParams(vmem_limit_bytes=limit),
            cost_estimate=pl.CostEstimate(flops=flops, bytes_accessed=4 * area, transcendentals=exps),
        )(*args)

    def column(n):
        return pltpu.VMEM((n, 1), f32)

    def line(n):
        return pltpu.VMEM((1, n), f32)

    flops = 2 * area * width
    source_line, target_line = source_order.reshape(1, rows), target_order.reshape(1, rows)
    order_block, row_block = pltpu.VMEM((1, rows), jnp.int32), pltpu.VMEM((rows, width), bf16)
    (sent,) = call(
        pack_kernel,
        [out((8, 2 * per, width), bf16)],
        [order_block, row_block, order_block, row_block, pltpu.SemaphoreType.DMA((4,))],
        [source_line, sources, target_line, targets],
        spec=hbm,
        limit=60 * 1024 * 1024,
    )
    got = across(sent)
    mine = got[:, :per].reshape(rows, width)
    aims = got[:, per:].reshape(rows, width)

    half = rows // 2
    s1 = swap(mine, "yl")
    s2 = swap(mine, "xl")
    t1 = swap(aims, "zl")
    t2 = swap(aims, "core")
    t3 = swap(t1, "core")
    s3a = swap(s2[:half], "yl")
    s3b = swap(s1[half:], "xl")
    matrix, all_sources, all_targets, part, norms = call(
        functools.partial(first_kernel, scale),
        [out((side, side), f32), out((side, width), bf16), out((side, width), bf16), out(tile, f32), out((1, side), f32)],
        [],
        [mine, s1, s2, aims, t1, t2, t3],
        3 * flops // 4,
        area,
    )
    matrix, all_sources, row_part = call(
        functools.partial(second_kernel, scale),
        [out((side, side), f32), out((side, width), bf16), out(tile, f32)],
        [],
        [all_targets, norms, part, s3a, s3b, matrix, all_sources],
        flops // 4,
        area // 4,
        {5: 0, 6: 1},
    )

    def exchange(value, slow, fast):
        both = swap(value, (slow, fast), ACROSS)
        second = swap(value, slow)
        first = swap(value, fast)
        return [value, first, second, both]

    for repeat in range(ITERS):
        column_part, source_potential = call(
            functools.partial(column_kernel, log_mass),
            [out(tile, f32), out(tile, f32)],
            [column(side)],
            [matrix] + exchange(row_part, "xl", "yl"),
            0,
            area,
        )
        column_parts = exchange(column_part, "core", "zl")
        if repeat < ITERS - 1:
            (row_part,) = call(
                functools.partial(row_kernel, log_mass),
                [out(tile, f32)],
                [line(side)],
                [matrix] + column_parts,
                0,
                area,
            )

    target_near, target_far = call(
        target_kernel,
        [out((2 * rows, width), bf16)] * 2,
        [column(side), line(side)],
        [matrix, all_sources, source_potential, column_part],
        flops,
        area,
    )
    near = swap(target_far, "core")
    made = {}
    lines = []
    for blocks in SPLIT:
        results = call(
            functools.partial(source_kernel, log_mass, blocks),
            [out((rows, width), bf16)] * len(blocks) + [out((tile[0] * len(blocks) // 4, LANES), f32)],
            [line(side)],
            [matrix, all_targets] + column_parts,
            flops * len(blocks) // 4,
            area * len(blocks) // 4,
        )
        made.update(zip(blocks, results))
        lines.append(results[-1])
    own_piece, piece_1, piece_2, piece_3 = [made[q] for q in range(4)]
    order = [q for blocks in SPLIT for q in blocks]
    joint = jnp.concatenate(lines, axis=0).reshape(4, -1, LANES)
    row_part = jnp.concatenate([joint[order.index(q)] for q in range(4)], axis=0)
    source_pieces = [own_piece, swap(piece_1, "yl"), swap(piece_2, "xl"), swap(piece_3, ("xl", "yl"), ACROSS)]
    row_parts = exchange(row_part, "xl", "yl")
    joined_own, joined_far = call(
        join_kernel, [out((rows, width), bf16)] * 2, [column(2 * rows)] * 2, [target_near, near] + column_parts
    )
    far = swap(joined_far, "zl")
    (back,) = call(
        finish_kernel,
        [out((8, 2 * per, width), bf16)],
        [column(rows)] * 4,
        [joined_own, far] + source_pieces + row_parts,
    )
    return call(
        unpack_kernel,
        [out((rows, width), bf16), out((rows, width), bf16)],
        [],
        [source_line, target_line, across(back)],
    )


def solution(mesh):
    split = Mesh(mesh.devices.reshape(SIZES), AXES)
    return jax.shard_map(
        whole,
        mesh=split,
        in_specs=(P(AXES, None), P(AXES, None), P(AXES), P(AXES)),
        out_specs=(P(AXES, None), P(AXES, None)),
        check_vma=False,
    )
```

```python
import functools
import itertools
import math

import jax
import jax.numpy as jnp
from jax import lax
from jax.experimental import pallas as pl
from jax.experimental.pallas import tpu as pltpu
from jax.sharding import Mesh, PartitionSpec as P


ITERS = 3
entropy_weight = 0.02
AXES = ("xh", "xl", "core", "zh", "zl", "yh", "yl")
SIZES = (2,) * 7
SWAP = [(0, 1), (1, 0)]
ACROSS = [(i, i ^ 3) for i in range(4)]
VMEM_LIMIT = 24 * 1024 * 1024
LANES = 128
STEP = 128
SPLIT = ((3,), (1,), (2, 0))


def compact(columns):
    lane = lax.broadcasted_iota(jnp.int32, (LANES, LANES), 1)
    held = jnp.zeros((LANES, LANES), jnp.float32)
    for n, column in enumerate(columns):
        held = jnp.where(lane == n, column, held)
    return jnp.transpose(held)[0 : len(columns)]


def combine(parts):
    highest = functools.reduce(jnp.maximum, parts)
    total = functools.reduce(jnp.add, [jnp.exp2(part - highest) for part in parts])
    return highest + jnp.log2(total)


def flip(part, q):
    per = part.shape[0] // 4
    return jnp.concatenate([part[(p ^ q) * per : ((p ^ q) + 1) * per] for p in range(4)], axis=0)


def aligned(parts):
    return [part if q == 0 else flip(part, q) for q, part in enumerate(parts)]


def put_row(row_ref, value):
    for a in range(value.shape[0]):
        row_ref[0:1, a * LANES : (a + 1) * LANES] = value[a : a + 1]


def put_column(column_ref, value):
    column_ref[:, 0 : value.shape[0]] = jnp.transpose(value)


def column_of(column_ref, a, count):
    n, b = a // LANES, a % LANES
    return column_ref[b : b + count, n : n + 1]


def over_blocks(column_ref, rows, make):
    return jnp.concatenate([make(a, column_of(column_ref, a, LANES)) for a in range(0, rows, LANES)], axis=0)


def row_lse_chunk(scores):
    highest = jnp.max(scores, axis=1, keepdims=True)
    total = jnp.sum(jnp.exp2(scores - highest), axis=1, keepdims=True)
    return highest + jnp.log2(total)


def pack_kernel(so_hbm, s_hbm, to_hbm, t_hbm, out_ref, so_ref, s_ref, to_ref, t_ref, sems):
    copies = [
        pltpu.make_async_copy(source, target, sems.at[n])
        for n, (source, target) in enumerate(
            ((so_hbm, so_ref), (s_hbm, s_ref), (to_hbm, to_ref), (t_hbm, t_ref))
        )
    ]
    for copy in copies:
        copy.start()
    rows = s_ref.shape[0]
    per = rows // 8
    slots = lax.broadcasted_iota(jnp.int32, (rows, rows), 0)
    for part, (order, matrix) in enumerate(((so_ref, s_ref), (to_ref, t_ref))):
        copies[2 * part].wait()
        copies[2 * part + 1].wait()
        chosen = jnp.where(slots == order[...], 1.0, 0.0).astype(jnp.bfloat16)
        moved = jnp.dot(chosen, matrix[...], preferred_element_type=jnp.float32).astype(jnp.bfloat16)
        for k in range(8):
            out_ref[k, part * per : (part + 1) * per, :] = moved[k * per : (k + 1) * per]


def unpack_kernel(so_ref, to_ref, back_ref, s_ref, t_ref):
    rows = s_ref.shape[0]
    per = rows // 8
    slots = lax.broadcasted_iota(jnp.int32, (rows, rows), 0)
    for part, (order, out) in enumerate(((so_ref, s_ref), (to_ref, t_ref))):
        chosen = jnp.where(slots == order[...], 1.0, 0.0).astype(jnp.bfloat16)
        moved = back_ref[:, part * per : (part + 1) * per, :].reshape(rows, out.shape[1])
        out[...] = lax.dot_general(
            chosen, moved, (((0,), (0,)), ((), ())), preferred_element_type=jnp.float32
        ).astype(jnp.bfloat16)


def target_norms(norm_ref, block, start):
    width = block.shape[1]
    for a in range(0, block.shape[0], LANES):
        wide = block[a : a + LANES, :].astype(jnp.float32)
        square = wide * wide
        folded = functools.reduce(jnp.add, [square[:, c : c + LANES] for c in range(0, width, LANES)])
        norm_ref[0:1, start + a : start + a + LANES] = jnp.sum(jnp.transpose(folded), axis=0, keepdims=True)


def score_rows(scale, rows, x_ref, y_ref, line_ref, m_ref, lse_ref):
    found = []
    for a in rows:
        block = x_ref[a : a + STEP, :]
        wide = block.astype(jnp.float32)
        norms = jnp.sum(wide * wide, axis=1, keepdims=True)
        inner = lax.dot_general(block, y_ref[...], (((1,), (1,)), ((), ())), preferred_element_type=jnp.float32)
        scores = (2.0 * inner - norms - line_ref[...]) * scale
        m_ref[a : a + STEP, :] = scores
        found.append(row_lse_chunk(scores))
    first = rows[0] // LANES
    lse_ref[first : first + len(found), :] = compact(found)


def first_kernel(scale, s0, s1, s2, t0, t1, t2, t3, m_ref, x_ref, y_ref, lse_ref, line_ref):
    rows = s0.shape[0]
    for q, s in enumerate((s0, s1, s2)):
        x_ref[q * rows : (q + 1) * rows, :] = s[...]
    for q, t in enumerate((t0, t1, t2, t3)):
        y_ref[q * rows : (q + 1) * rows, :] = t[...]
        target_norms(line_ref, t, q * rows)
    score_rows(scale, range(0, 3 * rows, STEP), x_ref, y_ref, line_ref, m_ref, lse_ref)


def second_kernel(scale, ready, y_ref, line_ref, part_ref, sb, m_in, x_in, m_ref, x_ref, lse_ref):
    half = sb.shape[0]
    x_ref[ready : ready + half, :] = sb[...]
    lse_ref[...] = part_ref[...]
    score_rows(scale, range(ready, ready + half, STEP), x_ref, y_ref, line_ref, m_ref, lse_ref)


def row_kernel(log_mass, m_ref, c0, c1, c2, c3, lse_ref, row_ref):
    put_row(row_ref, log_mass - combine(aligned([c0[...], c1[...], c2[...], c3[...]])))
    lse_ref[...] = compact(
        [row_lse_chunk(m_ref[a : a + STEP, :] + row_ref[...]) for a in range(0, m_ref.shape[0], STEP)]
    )


def column_kernel(log_mass, m_ref, r0, r1, r2, r3, lse_ref, f_ref, column_ref):
    potential = log_mass - combine(aligned([r0[...], r1[...], r2[...], r3[...]]))
    f_ref[...] = potential
    put_column(column_ref, potential)
    columns = m_ref.shape[1]
    step = 32

    def fold(values, op):
        return functools.reduce(op, [values[b : b + 8] for b in range(0, step, 8)])

    highest = jnp.full((8, columns), -jnp.inf, jnp.float32)
    for a in range(0, m_ref.shape[0], step):
        highest = jnp.maximum(highest, fold(m_ref[a : a + step, :] + column_of(column_ref, a, step), jnp.maximum))
    highest = jnp.max(highest, axis=0, keepdims=True)
    total = jnp.zeros((8, columns), jnp.float32)
    for a in range(0, m_ref.shape[0], step):
        scores = m_ref[a : a + step, :] + column_of(column_ref, a, step)
        total = total + fold(jnp.exp2(scores - highest), jnp.add)
    lse = highest + jnp.log2(jnp.sum(total, axis=0, keepdims=True))
    for a in range(lse_ref.shape[0]):
        lse_ref[a : a + 1, :] = lse[:, a * LANES : (a + 1) * LANES]


def target_kernel(first, m_ref, x_ref, f, c, out_ref, column_ref, row_ref):
    put_column(column_ref, f[...])
    put_row(row_ref, c[...])
    step = 256
    half = out_ref.shape[0]
    for b in range(0, half, step):
        a = first * half + b
        weights = over_blocks(
            column_ref,
            m_ref.shape[0],
            lambda c, column: jnp.exp2(
                m_ref[c : c + LANES, a : a + step] + column - row_ref[:, a : a + step]
            ).astype(jnp.bfloat16),
        )
        out_ref[b : b + step, :] = lax.dot_general(
            weights, x_ref[...], (((0,), (0,)), ((), ())), preferred_element_type=jnp.float32
        ).astype(jnp.bfloat16)


def source_kernel(log_mass, blocks, m_ref, y_ref, c0, c1, c2, c3, *refs):
    *pieces, lse_ref, row_ref = refs
    put_row(row_ref, log_mass - combine(aligned([c0[...], c1[...], c2[...], c3[...]])))
    rows = pieces[0].shape[0]
    found = []
    for place, a in enumerate(a for q in blocks for a in range(q * rows, (q + 1) * rows, STEP)):
        scores = m_ref[a : a + STEP, :] + row_ref[...]
        highest = jnp.max(scores, axis=1, keepdims=True)
        raised = jnp.exp2(scores - highest)
        total = jnp.sum(raised, axis=1, keepdims=True)
        mapped = jnp.dot(raised.astype(jnp.bfloat16), y_ref[...], preferred_element_type=jnp.float32)
        pieces[place * STEP // rows][a % rows : a % rows + STEP, :] = (mapped / total).astype(jnp.bfloat16)
        found.append(highest + jnp.log2(total))
    lse_ref[...] = compact(found)


def join_kernel(p_ref, near_ref, c0, c1, c2, c3, out_ref, far_ref, own_ref, mate_ref):
    rows = out_ref.shape[0]
    parts = aligned([c0[...], c1[...], c2[...], c3[...]])
    whole = combine(parts)
    top = whole.shape[0] // 2
    put_column(own_ref, jnp.exp2(parts[0] - whole)[:top])
    put_column(mate_ref, jnp.exp2(parts[2] - whole)[:top])
    joined = over_blocks(
        own_ref,
        2 * rows,
        lambda a, column: (
            p_ref[a : a + LANES, :].astype(jnp.float32) * column
            + near_ref[a : a + LANES, :].astype(jnp.float32) * column_of(mate_ref, a, LANES)
        ).astype(jnp.bfloat16),
    )
    out_ref[...] = joined[:rows]
    far_ref[...] = joined[rows:]


def finish_kernel(t_ref, far_ref, s0, s1, s2, s3, r0, r1, r2, r3, out_ref, w0, w1, w2, w3):
    rows = t_ref.shape[0]
    per = rows // 8
    parts = []
    for q, part in enumerate((r0, r1, r2, r3)):
        lines = part.shape[0] // 4
        parts.append(part[q * lines : (q + 1) * lines, :])
    whole = combine(parts)
    total = None
    for piece, part, column in zip((s0, s1, s2, s3), parts, (w0, w1, w2, w3)):
        put_column(column, jnp.exp2(part - whole))
        term = over_blocks(
            column, rows, lambda a, weight, piece=piece: piece[a : a + LANES, :].astype(jnp.float32) * weight
        )
        total = term if total is None else total + term
    total = total.astype(jnp.bfloat16)
    summed = (t_ref[...].astype(jnp.float32) + far_ref[...].astype(jnp.float32)).astype(jnp.bfloat16)
    for k in range(8):
        out_ref[k, 0:per, :] = total[k * per : (k + 1) * per]
        out_ref[k, per : 2 * per, :] = summed[k * per : (k + 1) * per]


def swap(value, axis, pairs=SWAP):
    return lax.ppermute(value, axis, pairs)


def place_of(xh, xl, core, zh, zl, yh, yl):
    index = 0
    for bit in (xh, xl, core, zh, zl, yh, yl):
        index = 2 * index + bit
    return index


def groups():
    return [
        [
            place_of(xh, gx ^ xh, core, zh, gz ^ zh, yh, gy ^ yh)
            for xh, zh, yh in itertools.product((0, 1), repeat=3)
        ]
        for gx, core, gz, gy in itertools.product((0, 1), repeat=4)
    ]


def across(value):
    return lax.all_to_all(value, AXES, split_axis=0, concat_axis=0, axis_index_groups=groups(), tiled=True)


def whole(sources, targets, source_order, target_order):
    rows, width = sources.shape
    side = 4 * rows
    per = rows // 8
    log_mass = -math.log2(4 * side)
    scale = 1.0 / (width * entropy_weight * math.log(2.0))
    vmem = pl.BlockSpec(memory_space=pltpu.VMEM)
    hbm = pl.BlockSpec(memory_space=pltpu.HBM)
    f32, bf16 = jnp.float32, jnp.bfloat16
    tile = (side // LANES, LANES)
    area = side * side

    def out(shape, dtype):
        return jax.ShapeDtypeStruct(shape, dtype)

    def call(kernel, outs, scratch, args, flops=0, exps=0, aliases=None, spec=vmem, limit=VMEM_LIMIT):
        return pl.pallas_call(
            kernel,
            out_shape=outs,
            in_specs=[spec] * len(args),
            out_specs=[vmem] * len(outs),
            scratch_shapes=scratch,
            input_output_aliases=aliases or {},
            compiler_params=pltpu.CompilerParams(vmem_limit_bytes=limit),
            cost_estimate=pl.CostEstimate(flops=flops, bytes_accessed=4 * area, transcendentals=exps),
        )(*args)

    def column(n):
        return pltpu.VMEM((LANES, n // LANES), f32)

    def line(n):
        return pltpu.VMEM((1, n), f32)

    flops = 2 * area * width
    source_line, target_line = source_order.reshape(1, rows), target_order.reshape(1, rows)
    order_block, row_block = pltpu.VMEM((1, rows), jnp.int32), pltpu.VMEM((rows, width), bf16)
    (sent,) = call(
        pack_kernel,
        [out((8, 2 * per, width), bf16)],
        [order_block, row_block, order_block, row_block, pltpu.SemaphoreType.DMA((4,))],
        [source_line, sources, target_line, targets],
        spec=hbm,
        limit=60 * 1024 * 1024,
    )
    got = across(sent)
    mine = got[:, :per].reshape(rows, width)
    aims = got[:, per:].reshape(rows, width)

    half = rows // 2
    s1 = swap(mine, "yl")
    s2 = swap(mine, "xl")
    t1 = swap(aims, "zl")
    t2 = swap(aims, "core")
    t3 = swap(t1, "core")
    s3a = swap(s2[:half], "yl")
    s3b = swap(s1[half:], "xl")
    matrix, all_sources, all_targets, part, norms = call(
        functools.partial(first_kernel, scale),
        [out((side, side), f32), out((side, width), bf16), out((side, width), bf16), out(tile, f32), out((1, side), f32)],
        [],
        [mine, s1, s2, aims, t1, t2, t3],
        3 * flops // 4,
        area,
    )
    row_part = part
    for ready, block in ((3 * rows + half, s3b), (3 * rows, s3a)):
        matrix, all_sources, row_part = call(
            functools.partial(second_kernel, scale, ready),
            [out((side, side), f32), out((side, width), bf16), out(tile, f32)],
            [],
            [all_targets, norms, row_part, block, matrix, all_sources],
            flops // 8,
            area // 8,
            {4: 0, 5: 1},
        )

    def exchange(value, slow, fast):
        both = swap(value, (slow, fast), ACROSS)
        second = swap(value, slow)
        first = swap(value, fast)
        return [value, first, second, both]

    for repeat in range(ITERS):
        column_part, source_potential = call(
            functools.partial(column_kernel, log_mass),
            [out(tile, f32), out(tile, f32)],
            [column(side)],
            [matrix] + exchange(row_part, "xl", "yl"),
            0,
            area,
        )
        column_parts = exchange(column_part, "core", "zl")
        if repeat < ITERS - 1:
            (row_part,) = call(
                functools.partial(row_kernel, log_mass),
                [out(tile, f32)],
                [line(side)],
                [matrix] + column_parts,
                0,
                area,
            )

    target_near, target_far = [
        call(
            functools.partial(target_kernel, first),
            [out((2 * rows, width), bf16)],
            [column(side), line(side)],
            [matrix, all_sources, source_potential, column_part],
            flops // 2,
            area // 2,
        )[0]
        for first in (0, 1)
    ]
    near = swap(target_far, "core")
    made = {}
    lines = []
    for blocks in SPLIT:
        results = call(
            functools.partial(source_kernel, log_mass, blocks),
            [out((rows, width), bf16)] * len(blocks) + [out((tile[0] * len(blocks) // 4, LANES), f32)],
            [line(side)],
            [matrix, all_targets] + column_parts,
            flops * len(blocks) // 4,
            area * len(blocks) // 4,
        )
        made.update(zip(blocks, results))
        lines.append(results[-1])
    own_piece, piece_1, piece_2, piece_3 = [made[q] for q in range(4)]
    order = [q for blocks in SPLIT for q in blocks]
    joint = jnp.concatenate(lines, axis=0).reshape(4, -1, LANES)
    row_part = jnp.concatenate([joint[order.index(q)] for q in range(4)], axis=0)
    source_pieces = [own_piece, swap(piece_1, "yl"), swap(piece_2, "xl"), swap(piece_3, ("xl", "yl"), ACROSS)]
    row_parts = exchange(row_part, "xl", "yl")
    joined_own, joined_far = call(
        join_kernel, [out((rows, width), bf16)] * 2, [column(2 * rows)] * 2, [target_near, near] + column_parts
    )
    far = swap(joined_far, "zl")
    (back,) = call(
        finish_kernel,
        [out((8, 2 * per, width), bf16)],
        [column(rows)] * 4,
        [joined_own, far] + source_pieces + row_parts,
    )
    return call(
        unpack_kernel,
        [out((rows, width), bf16), out((rows, width), bf16)],
        [],
        [source_line, target_line, across(back)],
    )


def solution(mesh):
    split = Mesh(mesh.devices.reshape(SIZES), AXES)
    return jax.shard_map(
        whole,
        mesh=split,
        in_specs=(P(AXES, None), P(AXES, None), P(AXES), P(AXES)),
        out_specs=(P(AXES, None), P(AXES, None)),
        check_vma=False,
    )
```

```python
import functools
import itertools
import math

import jax
import jax.numpy as jnp
from jax import lax
from jax.experimental import pallas as pl
from jax.experimental.pallas import tpu as pltpu
from jax.sharding import Mesh, PartitionSpec as P


ITERS = 3
entropy_weight = 0.02
AXES = ("xh", "xl", "core", "zh", "zl", "yh", "yl")
SIZES = (2,) * 7
SWAP = [(0, 1), (1, 0)]
ACROSS = [(i, i ^ 3) for i in range(4)]
VMEM_LIMIT = 24 * 1024 * 1024
LANES = 128
STEP = 128
SPLIT = ((3,), (1,), (2,), (0,))


def compact(columns):
    lane = lax.broadcasted_iota(jnp.int32, (LANES, LANES), 1)
    held = jnp.zeros((LANES, LANES), jnp.float32)
    for n, column in enumerate(columns):
        held = jnp.where(lane == n, column, held)
    return jnp.transpose(held)[0 : len(columns)]


def combine(parts):
    highest = functools.reduce(jnp.maximum, parts)
    total = functools.reduce(jnp.add, [jnp.exp2(part - highest) for part in parts])
    return highest + jnp.log2(total)


def flip(part, q):
    per = part.shape[0] // 4
    return jnp.concatenate([part[(p ^ q) * per : ((p ^ q) + 1) * per] for p in range(4)], axis=0)


def aligned(parts):
    return [part if q == 0 else flip(part, q) for q, part in enumerate(parts)]


def put_row(row_ref, value):
    for a in range(value.shape[0]):
        row_ref[0:1, a * LANES : (a + 1) * LANES] = value[a : a + 1]


def put_column(column_ref, value):
    column_ref[:, 0 : value.shape[0]] = jnp.transpose(value)


def column_of(column_ref, a, count):
    n, b = a // LANES, a % LANES
    return column_ref[b : b + count, n : n + 1]


def over_blocks(column_ref, rows, make):
    return jnp.concatenate([make(a, column_of(column_ref, a, LANES)) for a in range(0, rows, LANES)], axis=0)


def row_lse_chunk(scores):
    highest = jnp.max(scores, axis=1, keepdims=True)
    total = jnp.sum(jnp.exp2(scores - highest), axis=1, keepdims=True)
    return highest + jnp.log2(total)


def pack_kernel(so_hbm, s_hbm, to_hbm, t_hbm, out_ref, so_ref, s_ref, to_ref, t_ref, sems):
    copies = [
        pltpu.make_async_copy(source, target, sems.at[n])
        for n, (source, target) in enumerate(
            ((so_hbm, so_ref), (s_hbm, s_ref), (to_hbm, to_ref), (t_hbm, t_ref))
        )
    ]
    for copy in copies:
        copy.start()
    rows = s_ref.shape[0]
    per = rows // 8
    slots = lax.broadcasted_iota(jnp.int32, (rows, rows), 0)
    for part, (order, matrix) in enumerate(((so_ref, s_ref), (to_ref, t_ref))):
        copies[2 * part].wait()
        copies[2 * part + 1].wait()
        chosen = jnp.where(slots == order[...], 1.0, 0.0).astype(jnp.bfloat16)
        moved = jnp.dot(chosen, matrix[...], preferred_element_type=jnp.float32).astype(jnp.bfloat16)
        for k in range(8):
            out_ref[k, part * per : (part + 1) * per, :] = moved[k * per : (k + 1) * per]


def unpack_kernel(so_ref, to_ref, back_ref, s_ref, t_ref):
    rows = s_ref.shape[0]
    per = rows // 8
    slots = lax.broadcasted_iota(jnp.int32, (rows, rows), 0)
    for part, (order, out) in enumerate(((so_ref, s_ref), (to_ref, t_ref))):
        chosen = jnp.where(slots == order[...], 1.0, 0.0).astype(jnp.bfloat16)
        moved = back_ref[:, part * per : (part + 1) * per, :].reshape(rows, out.shape[1])
        out[...] = lax.dot_general(
            chosen, moved, (((0,), (0,)), ((), ())), preferred_element_type=jnp.float32
        ).astype(jnp.bfloat16)


def target_norms(norm_ref, block, start):
    width = block.shape[1]
    for a in range(0, block.shape[0], LANES):
        wide = block[a : a + LANES, :].astype(jnp.float32)
        square = wide * wide
        folded = functools.reduce(jnp.add, [square[:, c : c + LANES] for c in range(0, width, LANES)])
        norm_ref[0:1, start + a : start + a + LANES] = jnp.sum(jnp.transpose(folded), axis=0, keepdims=True)


def score_rows(scale, rows, x_ref, y_ref, line_ref, m_ref, lse_ref):
    found = []
    for a in rows:
        block = x_ref[a : a + STEP, :]
        wide = block.astype(jnp.float32)
        norms = jnp.sum(wide * wide, axis=1, keepdims=True)
        inner = lax.dot_general(block, y_ref[...], (((1,), (1,)), ((), ())), preferred_element_type=jnp.float32)
        scores = (2.0 * inner - norms - line_ref[...]) * scale
        m_ref[a : a + STEP, :] = scores
        found.append(row_lse_chunk(scores))
    first = rows[0] // LANES
    lse_ref[first : first + len(found), :] = compact(found)


def first_kernel(scale, s0, s1, s2, t0, t1, t2, t3, m_ref, x_ref, y_ref, lse_ref, line_ref):
    rows = s0.shape[0]
    for q, s in enumerate((s0, s1, s2)):
        x_ref[q * rows : (q + 1) * rows, :] = s[...]
    for q, t in enumerate((t0, t1, t2, t3)):
        y_ref[q * rows : (q + 1) * rows, :] = t[...]
        target_norms(line_ref, t, q * rows)
    score_rows(scale, range(0, 3 * rows, STEP), x_ref, y_ref, line_ref, m_ref, lse_ref)


def second_kernel(scale, y_ref, line_ref, part_ref, sa, sb, m_in, x_in, m_ref, x_ref, lse_ref):
    half = sa.shape[0]
    ready = 6 * half
    x_ref[ready : ready + half, :] = sa[...]
    x_ref[ready + half : ready + 2 * half, :] = sb[...]
    lines = ready // LANES
    lse_ref[0:lines, :] = part_ref[0:lines, :]
    score_rows(scale, range(ready, ready + 2 * half, STEP), x_ref, y_ref, line_ref, m_ref, lse_ref)


def row_kernel(log_mass, m_ref, c0, c1, c2, c3, lse_ref, row_ref):
    put_row(row_ref, log_mass - combine(aligned([c0[...], c1[...], c2[...], c3[...]])))
    lse_ref[...] = compact(
        [row_lse_chunk(m_ref[a : a + STEP, :] + row_ref[...]) for a in range(0, m_ref.shape[0], STEP)]
    )


def column_kernel(log_mass, m_ref, r0, r1, r2, r3, lse_ref, f_ref, column_ref):
    potential = log_mass - combine(aligned([r0[...], r1[...], r2[...], r3[...]]))
    f_ref[...] = potential
    put_column(column_ref, potential)
    columns = m_ref.shape[1]
    step = 32

    def fold(values, op):
        return functools.reduce(op, [values[b : b + 8] for b in range(0, step, 8)])

    highest = jnp.full((8, columns), -jnp.inf, jnp.float32)
    for a in range(0, m_ref.shape[0], step):
        highest = jnp.maximum(highest, fold(m_ref[a : a + step, :] + column_of(column_ref, a, step), jnp.maximum))
    highest = jnp.max(highest, axis=0, keepdims=True)
    total = jnp.zeros((8, columns), jnp.float32)
    for a in range(0, m_ref.shape[0], step):
        scores = m_ref[a : a + step, :] + column_of(column_ref, a, step)
        total = total + fold(jnp.exp2(scores - highest), jnp.add)
    lse = highest + jnp.log2(jnp.sum(total, axis=0, keepdims=True))
    for a in range(lse_ref.shape[0]):
        lse_ref[a : a + 1, :] = lse[:, a * LANES : (a + 1) * LANES]


def target_kernel(first, m_ref, x_ref, f, c, out_ref, column_ref, row_ref):
    put_column(column_ref, f[...])
    put_row(row_ref, c[...])
    step = 256
    half = out_ref.shape[0]
    for b in range(0, half, step):
        a = first * half + b
        weights = over_blocks(
            column_ref,
            m_ref.shape[0],
            lambda c, column: jnp.exp2(
                m_ref[c : c + LANES, a : a + step] + column - row_ref[:, a : a + step]
            ).astype(jnp.bfloat16),
        )
        out_ref[b : b + step, :] = lax.dot_general(
            weights, x_ref[...], (((0,), (0,)), ((), ())), preferred_element_type=jnp.float32
        ).astype(jnp.bfloat16)


def source_kernel(log_mass, blocks, m_ref, y_ref, c0, c1, c2, c3, *refs):
    *pieces, lse_ref, row_ref = refs
    put_row(row_ref, log_mass - combine(aligned([c0[...], c1[...], c2[...], c3[...]])))
    rows = pieces[0].shape[0]
    found = []
    for place, a in enumerate(a for q in blocks for a in range(q * rows, (q + 1) * rows, STEP)):
        scores = m_ref[a : a + STEP, :] + row_ref[...]
        highest = jnp.max(scores, axis=1, keepdims=True)
        raised = jnp.exp2(scores - highest)
        total = jnp.sum(raised, axis=1, keepdims=True)
        mapped = jnp.dot(raised.astype(jnp.bfloat16), y_ref[...], preferred_element_type=jnp.float32)
        pieces[place * STEP // rows][a % rows : a % rows + STEP, :] = (mapped / total).astype(jnp.bfloat16)
        found.append(highest + jnp.log2(total))
    lse_ref[...] = compact(found)


def join_kernel(p_ref, near_ref, c0, c1, c2, c3, out_ref, far_ref, own_ref, mate_ref):
    rows = out_ref.shape[0]
    parts = aligned([c0[...], c1[...], c2[...], c3[...]])
    whole = combine(parts)
    top = whole.shape[0] // 2
    put_column(own_ref, jnp.exp2(parts[0] - whole)[:top])
    put_column(mate_ref, jnp.exp2(parts[2] - whole)[:top])
    joined = over_blocks(
        own_ref,
        2 * rows,
        lambda a, column: (
            p_ref[a : a + LANES, :].astype(jnp.float32) * column
            + near_ref[a : a + LANES, :].astype(jnp.float32) * column_of(mate_ref, a, LANES)
        ).astype(jnp.bfloat16),
    )
    out_ref[...] = joined[:rows]
    far_ref[...] = joined[rows:]


def finish_kernel(t_ref, far_ref, s0, s1, s2, s3, r0, r1, r2, r3, out_ref, w0, w1, w2, w3):
    rows = t_ref.shape[0]
    per = rows // 8
    parts = []
    for q, part in enumerate((r0, r1, r2, r3)):
        lines = part.shape[0] // 4
        parts.append(part[q * lines : (q + 1) * lines, :])
    whole = combine(parts)
    total = None
    for piece, part, column in zip((s0, s1, s2, s3), parts, (w0, w1, w2, w3)):
        put_column(column, jnp.exp2(part - whole))
        term = over_blocks(
            column, rows, lambda a, weight, piece=piece: piece[a : a + LANES, :].astype(jnp.float32) * weight
        )
        total = term if total is None else total + term
    total = total.astype(jnp.bfloat16)
    summed = (t_ref[...].astype(jnp.float32) + far_ref[...].astype(jnp.float32)).astype(jnp.bfloat16)
    for k in range(8):
        out_ref[k, 0:per, :] = total[k * per : (k + 1) * per]
        out_ref[k, per : 2 * per, :] = summed[k * per : (k + 1) * per]


def swap(value, axis, pairs=SWAP):
    return lax.ppermute(value, axis, pairs)


def place_of(xh, xl, core, zh, zl, yh, yl):
    index = 0
    for bit in (xh, xl, core, zh, zl, yh, yl):
        index = 2 * index + bit
    return index


def groups():
    return [
        [
            place_of(xh, gx ^ xh, core, zh, gz ^ zh, yh, gy ^ yh)
            for xh, zh, yh in itertools.product((0, 1), repeat=3)
        ]
        for gx, core, gz, gy in itertools.product((0, 1), repeat=4)
    ]


def across(value):
    return lax.all_to_all(value, AXES, split_axis=0, concat_axis=0, axis_index_groups=groups(), tiled=True)


def whole(sources, targets, source_order, target_order):
    rows, width = sources.shape
    side = 4 * rows
    per = rows // 8
    log_mass = -math.log2(4 * side)
    scale = 1.0 / (width * entropy_weight * math.log(2.0))
    vmem = pl.BlockSpec(memory_space=pltpu.VMEM)
    hbm = pl.BlockSpec(memory_space=pltpu.HBM)
    f32, bf16 = jnp.float32, jnp.bfloat16
    tile = (side // LANES, LANES)
    area = side * side

    def out(shape, dtype):
        return jax.ShapeDtypeStruct(shape, dtype)

    def call(kernel, outs, scratch, args, flops=0, exps=0, aliases=None, spec=vmem, limit=VMEM_LIMIT):
        return pl.pallas_call(
            kernel,
            out_shape=outs,
            in_specs=[spec] * len(args),
            out_specs=[vmem] * len(outs),
            scratch_shapes=scratch,
            input_output_aliases=aliases or {},
            compiler_params=pltpu.CompilerParams(vmem_limit_bytes=limit),
            cost_estimate=pl.CostEstimate(flops=flops, bytes_accessed=4 * area, transcendentals=exps),
        )(*args)

    def column(n):
        return pltpu.VMEM((LANES, n // LANES), f32)

    def line(n):
        return pltpu.VMEM((1, n), f32)

    flops = 2 * area * width
    source_line, target_line = source_order.reshape(1, rows), target_order.reshape(1, rows)
    order_block, row_block = pltpu.VMEM((1, rows), jnp.int32), pltpu.VMEM((rows, width), bf16)
    (sent,) = call(
        pack_kernel,
        [out((8, 2 * per, width), bf16)],
        [order_block, row_block, order_block, row_block, pltpu.SemaphoreType.DMA((4,))],
        [source_line, sources, target_line, targets],
        spec=hbm,
        limit=60 * 1024 * 1024,
    )
    got = across(sent)
    mine = got[:, :per].reshape(rows, width)
    aims = got[:, per:].reshape(rows, width)

    half = rows // 2
    s1 = swap(mine, "yl")
    s2 = swap(mine, "xl")
    t1 = swap(aims, "zl")
    t2 = swap(aims, "core")
    t3 = swap(t1, "core")
    s3a = swap(s2[:half], "yl")
    s3b = swap(s1[half:], "xl")
    matrix, all_sources, all_targets, part, norms = call(
        functools.partial(first_kernel, scale),
        [out((side, side), f32), out((side, width), bf16), out((side, width), bf16), out(tile, f32), out((1, side), f32)],
        [],
        [mine, s1, s2, aims, t1, t2, t3],
        3 * flops // 4,
        area,
    )
    matrix, all_sources, row_part = call(
        functools.partial(second_kernel, scale),
        [out((side, side), f32), out((side, width), bf16), out(tile, f32)],
        [],
        [all_targets, norms, part, s3a, s3b, matrix, all_sources],
        flops // 4,
        area // 4,
        {5: 0, 6: 1},
    )

    def exchange(value, slow, fast):
        both = swap(value, (slow, fast), ACROSS)
        second = swap(value, slow)
        first = swap(value, fast)
        return [value, first, second, both]

    for repeat in range(ITERS):
        column_part, source_potential = call(
            functools.partial(column_kernel, log_mass),
            [out(tile, f32), out(tile, f32)],
            [column(side)],
            [matrix] + exchange(row_part, "xl", "yl"),
            0,
            area,
        )
        column_parts = exchange(column_part, "core", "zl")
        if repeat < ITERS - 1:
            (row_part,) = call(
                functools.partial(row_kernel, log_mass),
                [out(tile, f32)],
                [line(side)],
                [matrix] + column_parts,
                0,
                area,
            )

    target_near, target_far = [
        call(
            functools.partial(target_kernel, first),
            [out((2 * rows, width), bf16)],
            [column(side), line(side)],
            [matrix, all_sources, source_potential, column_part],
            flops // 2,
            area // 2,
        )[0]
        for first in (0, 1)
    ]
    near = swap(target_far, "core")
    made = {}
    lines = []
    for blocks in SPLIT:
        results = call(
            functools.partial(source_kernel, log_mass, blocks),
            [out((rows, width), bf16)] * len(blocks) + [out((tile[0] * len(blocks) // 4, LANES), f32)],
            [line(side)],
            [matrix, all_targets] + column_parts,
            flops * len(blocks) // 4,
            area * len(blocks) // 4,
        )
        made.update(zip(blocks, results))
        lines.append(results[-1])
    own_piece, piece_1, piece_2, piece_3 = [made[q] for q in range(4)]
    order = [q for blocks in SPLIT for q in blocks]
    joint = jnp.concatenate(lines, axis=0).reshape(4, -1, LANES)
    row_part = jnp.concatenate([joint[order.index(q)] for q in range(4)], axis=0)
    source_pieces = [own_piece, swap(piece_1, "yl"), swap(piece_2, "xl"), swap(piece_3, ("xl", "yl"), ACROSS)]
    row_parts = exchange(row_part, "xl", "yl")
    joined_own, joined_far = call(
        join_kernel, [out((rows, width), bf16)] * 2, [column(2 * rows)] * 2, [target_near, near] + column_parts
    )
    far = swap(joined_far, "zl")
    (back,) = call(
        finish_kernel,
        [out((8, 2 * per, width), bf16)],
        [column(rows)] * 4,
        [joined_own, far] + source_pieces + row_parts,
    )
    return call(
        unpack_kernel,
        [out((rows, width), bf16), out((rows, width), bf16)],
        [],
        [source_line, target_line, across(back)],
    )


def solution(mesh):
    split = Mesh(mesh.devices.reshape(SIZES), AXES)
    return jax.shard_map(
        whole,
        mesh=split,
        in_specs=(P(AXES, None), P(AXES, None), P(AXES), P(AXES)),
        out_specs=(P(AXES, None), P(AXES, None)),
        check_vma=False,
    )
```

```python
import functools
import itertools
import math

import jax
import jax.numpy as jnp
from jax import lax
from jax.experimental import pallas as pl
from jax.experimental.pallas import tpu as pltpu
from jax.sharding import Mesh, PartitionSpec as P


ITERS = 3
entropy_weight = 0.02
AXES = ("xh", "xl", "core", "zh", "zl", "yh", "yl")
SIZES = (2,) * 7
SWAP = [(0, 1), (1, 0)]
ACROSS = [(i, i ^ 3) for i in range(4)]
VMEM_LIMIT = 24 * 1024 * 1024
LANES = 128
STEP = 128
SPLIT = ((3,), (1,), (2,), (0,))


def compact(columns):
    lane = lax.broadcasted_iota(jnp.int32, (LANES, LANES), 1)
    held = jnp.zeros((LANES, LANES), jnp.float32)
    for n, column in enumerate(columns):
        held = jnp.where(lane == n, column, held)
    return jnp.transpose(held)[0 : len(columns)]


def combine(parts):
    highest = functools.reduce(jnp.maximum, parts)
    total = functools.reduce(jnp.add, [jnp.exp2(part - highest) for part in parts])
    return highest + jnp.log2(total)


def flip(part, q):
    per = part.shape[0] // 4
    return jnp.concatenate([part[(p ^ q) * per : ((p ^ q) + 1) * per] for p in range(4)], axis=0)


def aligned(parts):
    return [part if q == 0 else flip(part, q) for q, part in enumerate(parts)]


def put_row(row_ref, value):
    for a in range(value.shape[0]):
        row_ref[0:1, a * LANES : (a + 1) * LANES] = value[a : a + 1]


def put_column(column_ref, value):
    column_ref[:, 0 : value.shape[0]] = jnp.transpose(value)


def column_of(column_ref, a, count):
    n, b = a // LANES, a % LANES
    return column_ref[b : b + count, n : n + 1]


def over_blocks(column_ref, rows, make):
    return jnp.concatenate([make(a, column_of(column_ref, a, LANES)) for a in range(0, rows, LANES)], axis=0)


def row_lse_chunk(scores):
    highest = jnp.max(scores, axis=1, keepdims=True)
    total = jnp.sum(jnp.exp2(scores - highest), axis=1, keepdims=True)
    return highest + jnp.log2(total)


def pack_kernel(so_hbm, s_hbm, to_hbm, t_hbm, out_ref, so_ref, s_ref, to_ref, t_ref, sems):
    copies = [
        pltpu.make_async_copy(source, target, sems.at[n])
        for n, (source, target) in enumerate(
            ((so_hbm, so_ref), (s_hbm, s_ref), (to_hbm, to_ref), (t_hbm, t_ref))
        )
    ]
    for copy in copies:
        copy.start()
    rows = s_ref.shape[0]
    per = rows // 8
    slots = lax.broadcasted_iota(jnp.int32, (rows, rows), 0)
    for part, (order, matrix) in enumerate(((so_ref, s_ref), (to_ref, t_ref))):
        copies[2 * part].wait()
        copies[2 * part + 1].wait()
        chosen = jnp.where(slots == order[...], 1.0, 0.0).astype(jnp.bfloat16)
        moved = jnp.dot(chosen, matrix[...], preferred_element_type=jnp.float32).astype(jnp.bfloat16)
        for k in range(8):
            out_ref[k, part * per : (part + 1) * per, :] = moved[k * per : (k + 1) * per]


def unpack_kernel(so_ref, to_ref, back_ref, s_ref, t_ref):
    rows = s_ref.shape[0]
    per = rows // 8
    slots = lax.broadcasted_iota(jnp.int32, (rows, rows), 0)
    for part, (order, out) in enumerate(((so_ref, s_ref), (to_ref, t_ref))):
        chosen = jnp.where(slots == order[...], 1.0, 0.0).astype(jnp.bfloat16)
        moved = back_ref[:, part * per : (part + 1) * per, :].reshape(rows, out.shape[1])
        out[...] = lax.dot_general(
            chosen, moved, (((0,), (0,)), ((), ())), preferred_element_type=jnp.float32
        ).astype(jnp.bfloat16)


def target_norms(norm_ref, block, start):
    width = block.shape[1]
    for a in range(0, block.shape[0], LANES):
        wide = block[a : a + LANES, :].astype(jnp.float32)
        square = wide * wide
        folded = functools.reduce(jnp.add, [square[:, c : c + LANES] for c in range(0, width, LANES)])
        norm_ref[0:1, start + a : start + a + LANES] = jnp.sum(jnp.transpose(folded), axis=0, keepdims=True)


def score_rows(scale, rows, x_ref, y_ref, line_ref, m_ref, lse_ref):
    found = []
    for a in rows:
        block = x_ref[a : a + STEP, :]
        wide = block.astype(jnp.float32)
        norms = jnp.sum(wide * wide, axis=1, keepdims=True)
        inner = lax.dot_general(block, y_ref[...], (((1,), (1,)), ((), ())), preferred_element_type=jnp.float32)
        scores = (2.0 * inner - norms - line_ref[...]) * scale
        m_ref[a : a + STEP, :] = scores
        found.append(row_lse_chunk(scores))
    first = rows[0] // LANES
    lse_ref[first : first + len(found), :] = compact(found)


def first_kernel(scale, s0, s1, s2, t0, t1, t23, m_ref, x_ref, y_ref, lse_ref, line_ref):
    rows = s0.shape[0]
    for q, s in enumerate((s0, s1, s2)):
        x_ref[q * rows : (q + 1) * rows, :] = s[...]
    for q, t in enumerate((t0, t1, t23.at[pl.ds(0, rows)], t23.at[pl.ds(rows, rows)])):
        y_ref[q * rows : (q + 1) * rows, :] = t[...]
        target_norms(line_ref, t, q * rows)
    score_rows(scale, range(0, 3 * rows, STEP), x_ref, y_ref, line_ref, m_ref, lse_ref)


def second_kernel(scale, y_ref, line_ref, part_ref, sa, sb, m_in, x_in, m_ref, x_ref, lse_ref):
    half = sa.shape[0]
    ready = 6 * half
    x_ref[ready : ready + half, :] = sa[...]
    x_ref[ready + half : ready + 2 * half, :] = sb[...]
    lines = ready // LANES
    lse_ref[0:lines, :] = part_ref[0:lines, :]
    score_rows(scale, range(ready, ready + 2 * half, STEP), x_ref, y_ref, line_ref, m_ref, lse_ref)


def row_kernel(log_mass, m_ref, c0, c1, c2, c3, lse_ref, row_ref):
    put_row(row_ref, log_mass - combine(aligned([c0[...], c1[...], c2[...], c3[...]])))
    lse_ref[...] = compact(
        [row_lse_chunk(m_ref[a : a + STEP, :] + row_ref[...]) for a in range(0, m_ref.shape[0], STEP)]
    )


def column_kernel(log_mass, m_ref, r0, r1, r2, r3, lse_ref, f_ref, column_ref):
    potential = log_mass - combine(aligned([r0[...], r1[...], r2[...], r3[...]]))
    f_ref[...] = potential
    put_column(column_ref, potential)
    columns = m_ref.shape[1]
    step = 32

    def fold(values, op):
        return functools.reduce(op, [values[b : b + 8] for b in range(0, step, 8)])

    highest = jnp.full((8, columns), -jnp.inf, jnp.float32)
    for a in range(0, m_ref.shape[0], step):
        highest = jnp.maximum(highest, fold(m_ref[a : a + step, :] + column_of(column_ref, a, step), jnp.maximum))
    highest = jnp.max(highest, axis=0, keepdims=True)
    total = jnp.zeros((8, columns), jnp.float32)
    for a in range(0, m_ref.shape[0], step):
        scores = m_ref[a : a + step, :] + column_of(column_ref, a, step)
        total = total + fold(jnp.exp2(scores - highest), jnp.add)
    lse = highest + jnp.log2(jnp.sum(total, axis=0, keepdims=True))
    for a in range(lse_ref.shape[0]):
        lse_ref[a : a + 1, :] = lse[:, a * LANES : (a + 1) * LANES]


def target_kernel(first, m_ref, x_ref, f, c, out_ref, column_ref, row_ref):
    put_column(column_ref, f[...])
    put_row(row_ref, c[...])
    step = 256
    half = out_ref.shape[0]
    for b in range(0, half, step):
        a = first * half + b
        weights = over_blocks(
            column_ref,
            m_ref.shape[0],
            lambda c, column: jnp.exp2(
                m_ref[c : c + LANES, a : a + step] + column - row_ref[:, a : a + step]
            ).astype(jnp.bfloat16),
        )
        out_ref[b : b + step, :] = lax.dot_general(
            weights, x_ref[...], (((0,), (0,)), ((), ())), preferred_element_type=jnp.float32
        ).astype(jnp.bfloat16)


def source_kernel(log_mass, blocks, m_ref, y_ref, c0, c1, c2, c3, *refs):
    *pieces, lse_ref, row_ref = refs
    put_row(row_ref, log_mass - combine(aligned([c0[...], c1[...], c2[...], c3[...]])))
    rows = pieces[0].shape[0]
    found = []
    for place, a in enumerate(a for q in blocks for a in range(q * rows, (q + 1) * rows, STEP)):
        scores = m_ref[a : a + STEP, :] + row_ref[...]
        highest = jnp.max(scores, axis=1, keepdims=True)
        raised = jnp.exp2(scores - highest)
        total = jnp.sum(raised, axis=1, keepdims=True)
        mapped = jnp.dot(raised.astype(jnp.bfloat16), y_ref[...], preferred_element_type=jnp.float32)
        pieces[place * STEP // rows][a % rows : a % rows + STEP, :] = (mapped / total).astype(jnp.bfloat16)
        found.append(highest + jnp.log2(total))
    lse_ref[...] = compact(found)


def join_kernel(p_ref, near_ref, c0, c1, c2, c3, out_ref, far_ref, own_ref, mate_ref):
    rows = out_ref.shape[0]
    parts = aligned([c0[...], c1[...], c2[...], c3[...]])
    whole = combine(parts)
    top = whole.shape[0] // 2
    put_column(own_ref, jnp.exp2(parts[0] - whole)[:top])
    put_column(mate_ref, jnp.exp2(parts[2] - whole)[:top])
    joined = over_blocks(
        own_ref,
        2 * rows,
        lambda a, column: (
            p_ref[a : a + LANES, :].astype(jnp.float32) * column
            + near_ref[a : a + LANES, :].astype(jnp.float32) * column_of(mate_ref, a, LANES)
        ).astype(jnp.bfloat16),
    )
    out_ref[...] = joined[:rows]
    far_ref[...] = joined[rows:]


def finish_kernel(t_ref, far_ref, s0, s1, s2, s3, r0, r1, r2, r3, out_ref, w0, w1, w2, w3):
    rows = t_ref.shape[0]
    per = rows // 8
    parts = []
    for q, part in enumerate((r0, r1, r2, r3)):
        lines = part.shape[0] // 4
        parts.append(part[q * lines : (q + 1) * lines, :])
    whole = combine(parts)
    total = None
    for piece, part, column in zip((s0, s1, s2, s3), parts, (w0, w1, w2, w3)):
        put_column(column, jnp.exp2(part - whole))
        term = over_blocks(
            column, rows, lambda a, weight, piece=piece: piece[a : a + LANES, :].astype(jnp.float32) * weight
        )
        total = term if total is None else total + term
    total = total.astype(jnp.bfloat16)
    summed = (t_ref[...].astype(jnp.float32) + far_ref[...].astype(jnp.float32)).astype(jnp.bfloat16)
    for k in range(8):
        out_ref[k, 0:per, :] = total[k * per : (k + 1) * per]
        out_ref[k, per : 2 * per, :] = summed[k * per : (k + 1) * per]


def swap(value, axis, pairs=SWAP):
    return lax.ppermute(value, axis, pairs)


def place_of(xh, xl, core, zh, zl, yh, yl):
    index = 0
    for bit in (xh, xl, core, zh, zl, yh, yl):
        index = 2 * index + bit
    return index


def groups():
    return [
        [
            place_of(xh, gx ^ xh, core, zh, gz ^ zh, yh, gy ^ yh)
            for xh, zh, yh in itertools.product((0, 1), repeat=3)
        ]
        for gx, core, gz, gy in itertools.product((0, 1), repeat=4)
    ]


def across(value):
    return lax.all_to_all(value, AXES, split_axis=0, concat_axis=0, axis_index_groups=groups(), tiled=True)


def whole(sources, targets, source_order, target_order):
    rows, width = sources.shape
    side = 4 * rows
    per = rows // 8
    log_mass = -math.log2(4 * side)
    scale = 1.0 / (width * entropy_weight * math.log(2.0))
    vmem = pl.BlockSpec(memory_space=pltpu.VMEM)
    hbm = pl.BlockSpec(memory_space=pltpu.HBM)
    f32, bf16 = jnp.float32, jnp.bfloat16
    tile = (side // LANES, LANES)
    area = side * side

    def out(shape, dtype):
        return jax.ShapeDtypeStruct(shape, dtype)

    def call(kernel, outs, scratch, args, flops=0, exps=0, aliases=None, spec=vmem, limit=VMEM_LIMIT):
        return pl.pallas_call(
            kernel,
            out_shape=outs,
            in_specs=[spec] * len(args),
            out_specs=[vmem] * len(outs),
            scratch_shapes=scratch,
            input_output_aliases=aliases or {},
            compiler_params=pltpu.CompilerParams(vmem_limit_bytes=limit),
            cost_estimate=pl.CostEstimate(flops=flops, bytes_accessed=4 * area, transcendentals=exps),
        )(*args)

    def column(n):
        return pltpu.VMEM((LANES, n // LANES), f32)

    def line(n):
        return pltpu.VMEM((1, n), f32)

    flops = 2 * area * width
    source_line, target_line = source_order.reshape(1, rows), target_order.reshape(1, rows)
    order_block, row_block = pltpu.VMEM((1, rows), jnp.int32), pltpu.VMEM((rows, width), bf16)
    (sent,) = call(
        pack_kernel,
        [out((8, 2 * per, width), bf16)],
        [order_block, row_block, order_block, row_block, pltpu.SemaphoreType.DMA((4,))],
        [source_line, sources, target_line, targets],
        spec=hbm,
        limit=60 * 1024 * 1024,
    )
    got = across(sent)
    mine = got[:, :per].reshape(rows, width)
    aims = got[:, per:].reshape(rows, width)

    half = rows // 2
    s1 = swap(mine, "yl")
    s2 = swap(mine, "xl")
    t1 = swap(aims, "zl")
    t23 = swap(jnp.concatenate([aims, t1], axis=0), "core")
    s3a = swap(s2[:half], "yl")
    s3b = swap(s1[half:], "xl")
    matrix, all_sources, all_targets, part, norms = call(
        functools.partial(first_kernel, scale),
        [out((side, side), f32), out((side, width), bf16), out((side, width), bf16), out(tile, f32), out((1, side), f32)],
        [],
        [mine, s1, s2, aims, t1, t23],
        3 * flops // 4,
        area,
    )
    matrix, all_sources, row_part = call(
        functools.partial(second_kernel, scale),
        [out((side, side), f32), out((side, width), bf16), out(tile, f32)],
        [],
        [all_targets, norms, part, s3a, s3b, matrix, all_sources],
        flops // 4,
        area // 4,
        {5: 0, 6: 1},
    )

    def exchange(value, slow, fast):
        both = swap(value, (slow, fast), ACROSS)
        second = swap(value, slow)
        first = swap(value, fast)
        return [value, first, second, both]

    for repeat in range(ITERS):
        column_part, source_potential = call(
            functools.partial(column_kernel, log_mass),
            [out(tile, f32), out(tile, f32)],
            [column(side)],
            [matrix] + exchange(row_part, "xl", "yl"),
            0,
            area,
        )
        column_parts = exchange(column_part, "core", "zl")
        if repeat < ITERS - 1:
            (row_part,) = call(
                functools.partial(row_kernel, log_mass),
                [out(tile, f32)],
                [line(side)],
                [matrix] + column_parts,
                0,
                area,
            )

    target_near, target_far = [
        call(
            functools.partial(target_kernel, first),
            [out((2 * rows, width), bf16)],
            [column(side), line(side)],
            [matrix, all_sources, source_potential, column_part],
            flops // 2,
            area // 2,
        )[0]
        for first in (0, 1)
    ]
    near = swap(target_far, "core")
    made = {}
    lines = []
    for blocks in SPLIT:
        results = call(
            functools.partial(source_kernel, log_mass, blocks),
            [out((rows, width), bf16)] * len(blocks) + [out((tile[0] * len(blocks) // 4, LANES), f32)],
            [line(side)],
            [matrix, all_targets] + column_parts,
            flops * len(blocks) // 4,
            area * len(blocks) // 4,
        )
        made.update(zip(blocks, results))
        lines.append(results[-1])
    own_piece, piece_1, piece_2, piece_3 = [made[q] for q in range(4)]
    order = [q for blocks in SPLIT for q in blocks]
    joint = jnp.concatenate(lines, axis=0).reshape(4, -1, LANES)
    row_part = jnp.concatenate([joint[order.index(q)] for q in range(4)], axis=0)
    source_pieces = [own_piece, swap(piece_1, "yl"), swap(piece_2, "xl"), swap(piece_3, ("xl", "yl"), ACROSS)]
    row_parts = exchange(row_part, "xl", "yl")
    joined_own, joined_far = call(
        join_kernel, [out((rows, width), bf16)] * 2, [column(2 * rows)] * 2, [target_near, near] + column_parts
    )
    far = swap(joined_far, "zl")
    (back,) = call(
        finish_kernel,
        [out((8, 2 * per, width), bf16)],
        [column(rows)] * 4,
        [joined_own, far] + source_pieces + row_parts,
    )
    return call(
        unpack_kernel,
        [out((rows, width), bf16), out((rows, width), bf16)],
        [],
        [source_line, target_line, across(back)],
    )


def solution(mesh):
    split = Mesh(mesh.devices.reshape(SIZES), AXES)
    return jax.shard_map(
        whole,
        mesh=split,
        in_specs=(P(AXES, None), P(AXES, None), P(AXES), P(AXES)),
        out_specs=(P(AXES, None), P(AXES, None)),
        check_vma=False,
    )
```
